32 devices in a mesh: dp: 4 (over x, core), mp: 8 (over z, y).
Axes of the slice: x: 2, y: 2, z: 4, core: 2. Of those that a mesh axis runs over, the one named last changes fastest.
Arguments:
- tokens: bfloat16 [2048, 2048], P('dp', 'mp'), may hold values from -6 to 6
- cotangent: bfloat16 [2048, 2048], P('dp', 'mp'), may hold values from -6 to 6
- segment_ids: int32 [4, 512], P('dp'), may hold values from 0 to 5, never falling along the last dimension, each value on 1 to 256 neighbouring positions
- attention_gain: bfloat16 [2048], P('mp'), may hold values from 0.5 to 1.5
- feedforward_gain: bfloat16 [2048], P('mp'), may hold values from 0.5 to 1.5
- query_weight: bfloat16 [2048, 2048], P('mp'), may hold values from -0.125 to 0.125
- key_weight: bfloat16 [2048, 2048], P('mp'), may hold values from -0.125 to 0.125
- value_weight: bfloat16 [2048, 2048], P('mp'), may hold values from -0.125 to 0.125
- output_weight: bfloat16 [2048, 2048], P('mp'), may hold values from -0.125 to 0.125
- gate_weight: bfloat16 [2048, 5632], P('mp'), may hold values from -0.125 to 0.125
- up_weight: bfloat16 [2048, 5632], P('mp'), may hold values from -0.125 to 0.125
- down_weight: bfloat16 [5632, 2048], P('mp'), may hold values from -0.078125 to 0.078125
- query_left: float32 [2048, 16], P('mp'), may hold values from -0.125 to 0.125
- query_right: float32 [16, 2048], replicated, may hold values from -0.3 to 0.3
- query_magnitude: float32 [2048], replicated, may hold values from 1 to 2.5
- key_left: float32 [2048, 16], P('mp'), may hold values from -0.125 to 0.125
- key_right: float32 [16, 2048], replicated, may hold values from -0.3 to 0.3
- key_magnitude: float32 [2048], replicated, may hold values from 1 to 2.5
- value_left: float32 [2048, 16], P('mp'), may hold values from -0.125 to 0.125
- value_right: float32 [16, 2048], replicated, may hold values from -0.3 to 0.3
- value_magnitude: float32 [2048], replicated, may hold values from 0.5 to 1.5
- output_left: float32 [2048, 16], P('mp'), may hold values from -0.125 to 0.125
- output_right: float32 [16, 2048], replicated, may hold values from -0.3 to 0.3
- output_magnitude: float32 [2048], replicated, may hold values from 4 to 16
- gate_left: float32 [2048, 16], P('mp'), may hold values from -0.125 to 0.125
- gate_right: float32 [16, 5632], replicated, may hold values from -0.3 to 0.3
- gate_magnitude: float32 [5632], replicated, may hold values from 0.5 to 1.5
- up_left: float32 [2048, 16], P('mp'), may hold values from -0.125 to 0.125
- up_right: float32 [16, 5632], replicated, may hold values from -0.3 to 0.3
- up_magnitude: float32 [5632], replicated, may hold values from 0.5 to 1.5
- down_left: float32 [5632, 16], P('mp'), may hold values from -0.078125 to 0.078125
- down_right: float32 [16, 2048], replicated, may hold values from -0.3 to 0.3
- down_magnitude: float32 [2048], replicated, may hold values from 0.5 to 1.5
Outputs:
- layer_out: bfloat16 [2048, 2048], P('dp', 'mp')
- input_gradient: float32 [2048, 2048], P('dp', 'mp')
- query_left_gradient: float32 [2048, 16], P('mp')
- query_right_gradient: float32 [16, 2048], P(None, 'mp')
- query_magnitude_gradient: float32 [2048], P('mp')
- key_left_gradient: float32 [2048, 16], P('mp')
- key_right_gradient: float32 [16, 2048], P(None, 'mp')
- key_magnitude_gradient: float32 [2048], P('mp')
- value_left_gradient: float32 [2048, 16], P('mp')
- value_right_gradient: float32 [16, 2048], P(None, 'mp')
- value_magnitude_gradient: float32 [2048], P('mp')
- output_left_gradient: float32 [2048, 16], P('mp')
- output_right_gradient: float32 [16, 2048], P(None, 'mp')
- output_magnitude_gradient: float32 [2048], P('mp')
- gate_left_gradient: float32 [2048, 16], P('mp')
- gate_right_gradient: float32 [16, 5632], P(None, 'mp')
- gate_magnitude_gradient: float32 [5632], P('mp')
- up_left_gradient: float32 [2048, 16], P('mp')
- up_right_gradient: float32 [16, 5632], P(None, 'mp')
- up_magnitude_gradient: float32 [5632], P('mp')
- down_left_gradient: float32 [5632, 16], P('mp')
- down_right_gradient: float32 [16, 2048], P(None, 'mp')
- down_magnitude_gradient: float32 [2048], P('mp')
- statistics: float32 [7, 2], replicated
The draws below stay inside these ranges and needn't reach their ends.
Inputs may be any that keep to these rules, and one draw needn't show every extreme that they name: `segment_ids`: segment numbers never fall along a row; each row holds 6 segments, none empty, none longer than 256 tokens.
All inputs are finite; a program needn't handle non-finite values.
Results may differ from the reference program's by a relative error of at most 0.012.
The reference program's roundings to bfloat16 on the way count: a program that leaves them out, or rounds other values in their place, can miss the bound.
Values may be sent and summed in bfloat16 or wider, within the bound.
No kernel may reach another device: no remote copies, remote signals or barrier semaphores. Data moves between devices by JAX's collectives and lax.ppermute only.
A program may use at most 256 MiB of HBM per device.

```python
import math
import jax
import jax.numpy as jnp
import numpy as np
from jax import lax

D = 2048
H = 16
HD = 128
FF = 5632
R = 16
ALPHA = 32
SEQ = 512
SEGS = 6
ROWS = 4
TOKENS = 2048


def block_levels(own_key, dims, cuts, least, top_value):
    factor_of, own = 1.0, jax.random.fold_in(own_key, 6)
    for axis_at, shards_of in cuts:
        steps = jnp.exp(jax.random.uniform(jax.random.fold_in(own, axis_at), (shards_of,), jnp.float32, least / len(cuts), top_value / len(cuts)))
        factor_of = factor_of * jnp.repeat(steps, dims[axis_at] // shards_of).reshape([-1 if axis == axis_at else 1 for axis in range(len(dims))])
    return factor_of


def split_up(amount, total, most, slope):
    weights = [(1 << 20) // math.isqrt(grade ** slope) + 1 for grade in range(2, amount + 1)]
    surplus, holding = total - most - (amount - 1), [1] * (amount - 1)
    while surplus > 0:
        free = [i for i in range(amount - 1) if holding[i] < most]
        pool, budget = sum([weights[i] for i in free]), surplus
        for i in free:
            addition = min(most - holding[i], max(1, budget * weights[i] // pool), surplus)
            holding[i] = holding[i] + addition
            surplus = surplus - addition
    return np.array([most] + holding)


def uneven_parts(rng, amount, total, bound, lean):
    if amount == 2:
        one = jax.random.randint(rng, (), max(1, total - bound), min(bound, total - 1) + 1)
        return jnp.stack([one, total - one])
    sizes = jnp.asarray(split_up(amount, total, bound, lean), jnp.int32)
    pairs = (amount - 1) // 2
    giver, taker = sizes[1:1 + 2 * pairs:2], sizes[2:2 + 2 * pairs:2]
    slack = jnp.minimum(giver - 1, bound - taker)
    passed = jax.random.randint(jax.random.fold_in(rng, 1), (pairs,), 0, 1 << 20) % (slack + 1)
    sizes = sizes.at[1:1 + 2 * pairs:2].set(giver - passed).at[2:2 + 2 * pairs:2].set(taker + passed)
    return sizes[jax.random.permutation(jax.random.fold_in(rng, 2), amount)]


def normal_values(stream_key, extent, spread, most, shards=(), kind=jnp.bfloat16):
    factor_of = block_levels(stream_key, extent, shards, -0.22, 0.18) if shards else 1.0
    drawn = jax.random.normal(stream_key, extent, jnp.float32) * spread * factor_of
    return jnp.minimum(jnp.maximum(drawn, -most), most).astype(kind)


def setup_inputs(seed: int = 0) -> dict:
    arg_keys = jax.random.split(jax.random.key(seed), 34)
    return {
        "tokens": normal_values(arg_keys[0], (TOKENS, D), 1.0, 6.0, ((0, 4), (1, 8))),
        "cotangent": normal_values(arg_keys[1], (TOKENS, D), 1.0, 6.0, ((0, 4), (1, 8))),
        "segment_ids": jax.vmap(lambda own: jnp.searchsorted(jnp.cumsum(uneven_parts(own, SEGS, SEQ, SEQ // 2, 2)), jnp.arange(SEQ), side="right"))(jax.random.split(arg_keys[2], ROWS)).reshape((ROWS, SEQ)).astype(jnp.int32),
        "attention_gain": jnp.clip(1.0 + 0.1 * jax.random.normal(arg_keys[3], (D,), jnp.float32), 0.5, 1.5).astype(jnp.bfloat16),
        "feedforward_gain": jnp.clip(1.0 + 0.1 * jax.random.normal(arg_keys[4], (D,), jnp.float32), 0.5, 1.5).astype(jnp.bfloat16),
        "query_weight": normal_values(arg_keys[5], (D, D), D ** -0.5, 0.125, ((0, 8),)),
        "key_weight": normal_values(arg_keys[6], (D, D), D ** -0.5, 0.125, ((0, 8),)),
        "value_weight": normal_values(arg_keys[7], (D, D), D ** -0.5, 0.125, ((0, 8),)),
        "output_weight": normal_values(arg_keys[8], (D, D), D ** -0.5, 0.125, ((0, 8),)),
        "gate_weight": normal_values(arg_keys[9], (D, FF), D ** -0.5, 0.125, ((0, 8),)),
        "up_weight": normal_values(arg_keys[10], (D, FF), D ** -0.5, 0.125, ((0, 8),)),
        "down_weight": normal_values(arg_keys[11], (FF, D), FF ** -0.5, 0.078125, ((0, 8),)),
        "query_left": normal_values(arg_keys[12], (D, R), D ** -0.5, 0.125, ((0, 8),), jnp.float32),
        "query_right": normal_values(arg_keys[13], (R, D), 0.05, 0.3, (), jnp.float32),
        "query_magnitude": jnp.clip(jnp.exp(jax.random.uniform(arg_keys[14], (D,), jnp.float32, math.log(1.0), math.log(2.5))), 1.0, 2.5),
        "key_left": normal_values(arg_keys[15], (D, R), D ** -0.5, 0.125, ((0, 8),), jnp.float32),
        "key_right": normal_values(arg_keys[16], (R, D), 0.05, 0.3, (), jnp.float32),
        "key_magnitude": jnp.clip(jnp.exp(jax.random.uniform(arg_keys[17], (D,), jnp.float32, math.log(1.0), math.log(2.5))), 1.0, 2.5),
        "value_left": normal_values(arg_keys[18], (D, R), D ** -0.5, 0.125, ((0, 8),), jnp.float32),
        "value_right": normal_values(arg_keys[19], (R, D), 0.05, 0.3, (), jnp.float32),
        "value_magnitude": jnp.clip(1.0 + 0.1 * jax.random.normal(arg_keys[20], (D,), jnp.float32), 0.5, 1.5),
        "output_left": normal_values(arg_keys[21], (D, R), D ** -0.5, 0.125, ((0, 8),), jnp.float32),
        "output_right": normal_values(arg_keys[22], (R, D), 0.05, 0.3, (), jnp.float32),
        "output_magnitude": jnp.clip(jnp.exp(jax.random.uniform(arg_keys[23], (D,), jnp.float32, math.log(4.0), math.log(16.0))), 4.0, 16.0),
        "gate_left": normal_values(arg_keys[24], (D, R), D ** -0.5, 0.125, ((0, 8),), jnp.float32),
        "gate_right": normal_values(arg_keys[25], (R, FF), 0.05, 0.3, (), jnp.float32),
        "gate_magnitude": jnp.clip(1.0 + 0.1 * jax.random.normal(arg_keys[26], (FF,), jnp.float32), 0.5, 1.5),
        "up_left": normal_values(arg_keys[27], (D, R), D ** -0.5, 0.125, ((0, 8),), jnp.float32),
        "up_right": normal_values(arg_keys[28], (R, FF), 0.05, 0.3, (), jnp.float32),
        "up_magnitude": jnp.clip(1.0 + 0.1 * jax.random.normal(arg_keys[29], (FF,), jnp.float32), 0.5, 1.5),
        "down_left": normal_values(arg_keys[30], (FF, R), FF ** -0.5, 0.078125, ((0, 8),), jnp.float32),
        "down_right": normal_values(arg_keys[31], (R, D), 0.05, 0.3, (), jnp.float32),
        "down_magnitude": jnp.clip(1.0 + 0.1 * jax.random.normal(arg_keys[32], (D,), jnp.float32), 0.5, 1.5),
    }


@jax.custom_vjp
def low(v):
    return lax.optimization_barrier(v.astype(jnp.bfloat16)).astype(jnp.float32)

@jax.custom_vjp
def low_back(v):
    return v

def low_keep(v):
    return (low(v), None)

def low_pass(kept, grad):
    return (grad,)

def back_keep(v):
    return (v, None)

def back_low(kept, grad):
    return (low(grad),)
low.defvjp(low_keep, low_pass)
low_back.defvjp(back_keep, back_low)
EPS = 1e-05
THETA = 10000.0
NEGATIVE = -1e+30

def precise(left_part, right_part):
    return jnp.dot(left_part, right_part, precision=lax.Precision.HIGHEST)

def rms_norm(values, gain):
    return values * lax.rsqrt(lax.optimization_barrier(jnp.mean(values * values, axis=-1, keepdims=True)) + EPS) * gain

def column_norms(weight, left_factor, right_factor):
    adapted_full = weight + ALPHA / R * precise(left_factor, right_factor)
    return jnp.sqrt(lax.optimization_barrier(jnp.sum(adapted_full * adapted_full, axis=0)))

def adapted(inputs, weight, left_factor, right_factor, magnitude):
    shaped = precise(inputs, weight) + ALPHA / R * precise(precise(inputs, left_factor), right_factor)
    shaped = low_back(shaped)
    return shaped * (magnitude / column_norms(weight, left_factor, right_factor))

def positions(segments):
    places = jnp.arange(SEQ, dtype=jnp.int32)
    change = jnp.concatenate([jnp.ones((1,), jnp.int32), (segments[1:] != segments[:-1]).astype(jnp.int32)])
    return places - lax.cummax(places * change, axis=0)

def rotary(values, places):
    half_dim = HD // 2
    freqs = THETA ** (-2.0 * jnp.arange(half_dim, dtype=jnp.float32) / HD)
    angles = places.astype(jnp.float32)[:, None] * freqs[None, :]
    cosine = jnp.cos(angles)[:, None, :]
    sine = jnp.sin(angles)[:, None, :]
    first_half = values[..., :half_dim]
    second_half = values[..., half_dim:]
    return jnp.concatenate([first_half * cosine - second_half * sine, second_half * cosine + first_half * sine], axis=-1)

def attend_row(items):
    queries, key_rows, value_rows, segments = items
    places = positions(segments)
    head_shape = (SEQ, H, HD)
    query_low = low(rotary(queries.reshape(head_shape), places))
    key_low = low(rotary(key_rows.reshape(head_shape), places))
    value_low = low(value_rows.reshape(head_shape))
    raw_scores = low_back(jnp.einsum('qhd,khd->hqk', query_low, key_low, precision=lax.Precision.HIGHEST))
    indices = jnp.arange(SEQ, dtype=jnp.int32)
    allowed = (segments[:, None] == segments[None, :]) & (indices[None, :] <= indices[:, None])
    logits = jnp.where(allowed[None], raw_scores * HD ** (-0.5), NEGATIVE)
    weights = low(jax.nn.softmax(logits, axis=-1))
    mixed = jnp.einsum('hqk,khd->qhd', weights, value_low, precision=lax.Precision.HIGHEST)
    return mixed.reshape(SEQ, D)

def layer(field, segments, gain_first, gain_second, weights, lefts, rights, magnitudes):
    normed = low(rms_norm(field, gain_first))
    projected = [adapted(normed, weights[member], lefts[member], rights[member], magnitudes[member]) for member in range(3)]
    row_shape = (ROWS, SEQ, D)
    attended = lax.map(jax.checkpoint(attend_row), (projected[0].reshape(row_shape), projected[1].reshape(row_shape), projected[2].reshape(row_shape), segments))
    attended = low(low_back(attended.reshape(TOKENS, D)))
    middle = field + adapted(attended, weights[3], lefts[3], rights[3], magnitudes[3])
    normed_two = low(rms_norm(middle, gain_second))
    gate = adapted(normed_two, weights[4], lefts[4], rights[4], magnitudes[4])
    upper = adapted(normed_two, weights[5], lefts[5], rights[5], magnitudes[5])
    activated = low(jax.nn.silu(gate) * upper)
    return middle + adapted(activated, weights[6], lefts[6], rights[6], magnitudes[6])

def reference(tokens, cotangent, segment_ids, attention_gain, feedforward_gain, query_weight, key_weight, value_weight, output_weight, gate_weight, up_weight, down_weight, query_left, query_right, query_magnitude, key_left, key_right, key_magnitude, value_left, value_right, value_magnitude, output_left, output_right, output_magnitude, gate_left, gate_right, gate_magnitude, up_left, up_right, up_magnitude, down_left, down_right, down_magnitude):
    weights = tuple((weight.astype(jnp.float32) for weight in (query_weight, key_weight, value_weight, output_weight, gate_weight, up_weight, down_weight)))
    lefts = (query_left, key_left, value_left, output_left, gate_left, up_left, down_left)
    rights = (query_right, key_right, value_right, output_right, gate_right, up_right, down_right)
    magnitudes = (query_magnitude, key_magnitude, value_magnitude, output_magnitude, gate_magnitude, up_magnitude, down_magnitude)
    gain_first = attention_gain.astype(jnp.float32)
    gain_second = feedforward_gain.astype(jnp.float32)

    def forward(field, left_set, right_set, magnitude_set):
        return layer(field, segment_ids, gain_first, gain_second, weights, left_set, right_set, magnitude_set)
    result, pullback = jax.vjp(forward, tokens.astype(jnp.float32), lefts, rights, magnitudes)
    grad_field, grad_lefts, grad_rights, grad_magnitudes = pullback(cotangent.astype(jnp.float32))
    rows_stats = []
    for member in range(7):
        norms = column_norms(weights[member], lefts[member], rights[member])
        drift = jnp.sqrt(jnp.mean((magnitudes[member] - norms) ** 2))
        rows_stats.append(jnp.stack([drift, jnp.mean(norms)]))
    statistics = jnp.stack(rows_stats)
    return (result.astype(jnp.bfloat16), grad_field, grad_lefts[0], grad_rights[0], grad_magnitudes[0], grad_lefts[1], grad_rights[1], grad_magnitudes[1], grad_lefts[2], grad_rights[2], grad_magnitudes[2], grad_lefts[3], grad_rights[3], grad_magnitudes[3], grad_lefts[4], grad_rights[4], grad_magnitudes[4], grad_lefts[5], grad_rights[5], grad_magnitudes[5], grad_lefts[6], grad_rights[6], grad_magnitudes[6], statistics)
```

```python
import jax
import jax.numpy as jnp
from jax import lax
from jax.experimental import pallas as pl
from jax.experimental.pallas import tpu as pltpu
from jax.sharding import PartitionSpec as P

HD = 128
R = 16
ALPHA = 32
SCALE = ALPHA / R
EPS = 1e-05
THETA = 10000.0
NEGATIVE = -1e30
PLANES = 4
CORES = 2
LOW = jnp.bfloat16
F32 = jnp.float32


def swap(values, offset, axis):
    count = lax.axis_size(axis)
    return lax.ppermute(values, axis, [(place, place ^ offset) for place in range(count)])


def gather(chunk):
    count = lax.axis_size("mp")
    inner = count // PLANES
    got = [None] * count
    got[0] = chunk
    for a in range(1, PLANES):
        got[a * inner] = swap(chunk, a * inner, "mp")
    for a in range(PLANES):
        for b in range(1, inner):
            got[a * inner + b] = swap(got[a * inner], b, "mp")
    return got


def total_over(values, axis):
    offset = 1
    while offset < lax.axis_size(axis):
        values = values + swap(values, offset, axis)
        offset *= 2
    return values


def small_gather(chunk):
    count = lax.axis_size("mp")
    inner = count // PLANES
    held = jnp.stack([chunk] + [swap(chunk, a * inner, "mp") for a in range(1, PLANES)])
    sides = [held] + [swap(held, b, "mp") for b in range(1, inner)]
    return jnp.concatenate([sides[k % inner][k // inner] for k in range(count)], axis=1)


def small_scatter(bundles):
    inner = len(bundles)
    held = bundles[0].astype(F32)
    for b in range(1, inner):
        held = held + swap(bundles[b], b, "mp").astype(F32)
    final = held[0]
    for a in range(1, PLANES):
        sent = held[a].astype(LOW)
        final = final + swap(sent, a * inner, "mp").astype(F32)
    return final


def total_relative(values):
    count = values.shape[0]
    offset = 1
    while offset < count:
        turned = jnp.stack([values[k ^ offset] for k in range(count)])
        values = values + swap(turned, offset, "mp")
        offset *= 2
    return values


def dot(left_part, right_part, left_dim=1, right_dim=0):
    return lax.dot_general(
        left_part,
        right_part,
        (((left_dim,), (right_dim,)), ((), ())),
        preferred_element_type=F32,
    )


def split(values):
    high = values.astype(LOW)
    return high, (values - high.astype(F32)).astype(LOW)


def split_rows(values):
    high = lax.reduce_precision(values, 8, 7)
    return jnp.concatenate([high, values - high], axis=0).astype(LOW)


def round_up(size):
    return -(-size // 128) * 128


def pad_to(values, size, axis):
    if values.shape[axis] == size:
        return values
    widths = [(0, 0)] * values.ndim
    widths[axis] = (0, size - values.shape[axis])
    return jnp.pad(values, widths)


def kernel(body, outs, *operands, scalars=None):
    specs = [pl.BlockSpec(memory_space=pltpu.VMEM)] * len(operands)
    if scalars is not None:
        specs = [pl.BlockSpec(memory_space=pltpu.SMEM)] + specs
        operands = (scalars,) + operands
    return pl.pallas_call(
        body,
        out_shape=tuple(jax.ShapeDtypeStruct(shape, kind) for shape, kind in outs),
        in_specs=specs,
    )(*operands)


def by_rows(body, steps, chunks, rowed, summed_outs, across, outs, *operands):
    def spec(shape, by_block):
        if by_block:
            return pl.BlockSpec((shape[0] // steps, shape[1]), lambda i: (i, 0))
        return pl.BlockSpec(shape, lambda i: (0, 0))

    out_specs = [spec(shape, slot not in summed_outs) for slot, (shape, _) in enumerate(outs)]
    if across is not None:
        shape = outs[across][0]
        out_specs[across] = pl.BlockSpec((shape[0], shape[1] // steps), lambda i: (0, i))
    return pl.pallas_call(
        body,
        grid=(steps,),
        in_specs=[
            spec(operand.shape, slot < chunks or slot in rowed)
            for slot, operand in enumerate(operands)
        ],
        out_specs=out_specs,
        out_shape=[jax.ShapeDtypeStruct(shape, kind) for shape, kind in outs],
    )(*operands)


def add_low(first, *others):
    def body(*refs):
        total = refs[0][...].astype(F32)
        for ref in refs[1:-1]:
            total = total + ref[...].astype(F32)
        refs[-1][...] = total.astype(LOW)

    return kernel(body, [(first.shape, LOW)], first, *others)[0]


def scatter_pieces(parts):
    count = len(parts)
    inner = count // PLANES
    order = list(range(1, PLANES)) + [0]
    got = {a: [swap(parts[a * inner + b], b, "mp") for b in range(1, inner)] for a in order}
    sent = [swap(add_low(parts[a * inner], *got[a]), a * inner, "mp") for a in order[:-1]]
    return [parts[0]] + got[0] + sent


def summed(refs):
    total = refs[0][...].astype(F32)
    for ref in refs[1:]:
        total = total + ref[...].astype(F32)
    return total


def take_columns(ref, taken, index, width, padded):
    start = index * width
    if width % 128 == 0:
        return ref[taken, pl.ds(pl.multiple_of(start, 128), width)]
    window = round_up(width + 127)
    base = pl.multiple_of(jnp.minimum((start >> 7) << 7, ref.shape[1] - window), 128)
    values = ref[taken, pl.ds(base, window)]
    turn = lax.rem(window - (start - base), window)
    turned = pltpu.roll(values.astype(F32), turn, axis=1)[:, :padded]
    lanes = lax.broadcasted_iota(jnp.int32, turned.shape, 1)
    return jnp.where(lanes < width, turned, 0.0).astype(values.dtype)


def own_factors(rights, magnitudes, width, hidden, padded, scalars):
    def body(place_ref, *refs):
        right_refs, magnitude_refs = refs[:5], refs[5:12]
        place = place_ref[0]
        for members, size, filled, pair_ref in (
            (range(3), width, width, refs[12]),
            (range(3, 5), hidden, padded, refs[13]),
        ):
            half = len(members) * R
            pair_ref[...] = jnp.zeros_like(pair_ref)
            for slot, member in enumerate(members):
                high, rest = split(
                    take_columns(right_refs[member], slice(None), place, size, filled)
                )
                rows = slice(slot * R, (slot + 1) * R)
                lanes = slice(slot * filled, (slot + 1) * filled)
                pair_ref[rows, lanes] = high
                pair_ref[half + slot * R : half + (slot + 1) * R, lanes] = rest
        taken = [
            take_columns(
                ref,
                slice(None),
                place,
                hidden if member in (4, 5) else width,
                padded if member in (4, 5) else width,
            )
            for member, ref in enumerate(magnitude_refs)
        ]
        for slot in range(3):
            refs[14][:, slot * width : (slot + 1) * width] = taken[slot]
        refs[15][:, :padded] = taken[4]
        refs[15][:, padded:] = taken[5]
        refs[16][...] = taken[3]
        refs[17][...] = taken[6]

    return kernel(
        body,
        [
            ((6 * R, 3 * width), LOW),
            ((4 * R, 2 * padded), LOW),
            ((1, 3 * width), F32),
            ((1, 2 * padded), F32),
            ((1, width), F32),
            ((1, width), F32),
        ],
        *[rights[member] for member in (0, 1, 2, 4, 5)],
        *[values[None] for values in magnitudes],
        scalars=scalars,
    )


def gathered_lefts(chunks, tokens):
    width = chunks[0].shape[1]

    def body(*refs):
        left_ref, gain_ref = refs[-2:]
        for k, ref in enumerate(refs[:-2]):
            lanes = slice(k * width, (k + 1) * width)
            left_ref[:, lanes] = ref[tokens : tokens + 6 * R, :]
            gain_ref[:, lanes] = ref[tokens + 6 * R : tokens + 6 * R + 16, :].astype(F32)[1:2]

    total = len(chunks) * width
    outs = [((6 * R, total), LOW), ((1, total), F32)]
    return kernel(body, outs, *chunks)


def cut_blocks(weights, width, padded, scalars):
    count = lax.axis_size("mp")
    members = len(weights)
    rows, _ = weights[0].shape
    part = rows // lax.axis_size("dp")

    def body(place_ref, *refs):
        sources, own_ref, block_refs = refs[:members], refs[members], refs[members + 1 :]
        place = place_ref[0]
        mine = pl.ds(pl.multiple_of(place_ref[1] * part, part), part)

        for slot, ref in enumerate(sources):
            lanes = slice(slot * padded, (slot + 1) * padded)
            own_ref[:, lanes] = take_columns(ref, slice(None), place, width, padded)
            for k in range(1, count):
                block_refs[k - 1][:, lanes] = take_columns(
                    ref, mine, place ^ k, width, padded
                )

    wide = members * padded
    return kernel(
        body, [((rows, wide), LOW)] + [((part, wide), LOW)] * (count - 1), *weights, scalars=scalars
    )


def bundled(blocks):
    def body(*refs):
        for slot, ref in enumerate(refs[:-1]):
            refs[-1][slot] = ref[...]

    shape = (len(blocks),) + blocks[0].shape
    return kernel(body, [(shape, LOW)], *blocks)[0]


def exchanged(blocks):
    bundle = bundled([swap(block, k + 1, "mp") for k, block in enumerate(blocks)])
    pieces = []
    for j in range(0, lax.axis_size("dp"), CORES):
        held = bundle if j == 0 else swap(bundle, j, "dp")
        pieces.append(held)
        pieces += [swap(held, c, "dp") for c in range(1, CORES)]
    return pieces


def thrice(pair, swapped):
    half = pair.shape[0] // 2
    high, rest = pair[:half], pair[half:]
    return jnp.concatenate([high, high, rest] if swapped else [high, rest, high], axis=0)


def assemble(own, pieces, lefts_all, rights_pair, scalars, keep):
    count = lax.axis_size("mp")
    rows, wide = own.shape
    part = pieces[0].shape[1]
    copies = len(pieces)

    def body(place_ref, own_ref, left_ref, right_ref, *refs):
        piece_refs, (weight_ref, full_ref, square_ref) = refs[:copies], refs[copies:]
        k = pl.program_id(0)

        @pl.when(k == 0)
        def _():
            weight_ref[...] = own_ref[...]
            square_ref[...] = jnp.zeros_like(square_ref)

        @pl.when(k > 0)
        def _():
            for j, ref in enumerate(piece_refs):
                at = pl.multiple_of((place_ref[1] ^ j) * part, part)
                weight_ref[pl.ds(at, part), :] = ref[0]

        full = weight_ref[...].astype(F32) + dot(
            thrice(left_ref[...], False), thrice(right_ref[...], True), 0, 0
        )
        full_ref[...] = full.astype(LOW)
        square_ref[...] += jnp.sum(full * full, axis=0, keepdims=True)

    whole = lambda k: (0, 0)

    def body_alone(*refs):
        body(*refs[: 4 + copies], refs[-1], *refs[4 + copies : -1])

    return pl.pallas_call(
        body if keep else body_alone,
        scratch_shapes=[] if keep else [pltpu.VMEM((rows, wide), LOW)],
        grid=(count,),
        in_specs=[
            pl.BlockSpec(memory_space=pltpu.SMEM),
            pl.BlockSpec((rows, wide), whole),
            pl.BlockSpec((lefts_all.shape[0], rows), lambda k: (0, k)),
            pl.BlockSpec(rights_pair.shape, whole),
        ]
        + [pl.BlockSpec((1, part, wide), lambda k: (jnp.maximum(k - 1, 0), 0, 0))] * len(pieces),
        out_specs=[pl.BlockSpec((rows, wide), lambda k: (k, 0))] * (2 if keep else 1)
        + [pl.BlockSpec((1, wide), whole)],
        out_shape=[jax.ShapeDtypeStruct((count * rows, wide), LOW)] * (2 if keep else 1)
        + [jax.ShapeDtypeStruct((1, wide), F32)],
    )(scalars, own, lefts_all, rights_pair, *pieces)


def row_block(weight, left_pair, right, magnitude, width, rows_padded, scalars):
    count = lax.axis_size("mp")
    rows, total = weight.shape

    def body(
        place_ref,
        weight_ref,
        left_ref,
        right_ref,
        magnitude_ref,
        full_ref,
        high_ref,
        square_ref,
        moved_ref,
        *cross_refs,
    ):
        lefts = thrice(left_ref[...], False)
        for k in range(count):
            at = pl.ds(pl.multiple_of((place_ref[0] ^ k) * width, width), width)
            lanes = slice(k * width, (k + 1) * width)
            values = weight_ref[:, at]
            if rows < rows_padded:
                fill = jnp.zeros((rows_padded - rows, width), LOW)
                values = jnp.concatenate([values, fill], axis=0)
            high, rest = split(right_ref[:, at])
            pair = jnp.concatenate([high, rest], axis=0)
            high_ref[:, lanes] = high
            moved_ref[:, lanes] = magnitude_ref[:, at]
            full = values.astype(F32) + dot(lefts, thrice(pair, True), 0, 0)
            low = full.astype(LOW)
            full_ref[:, lanes] = low
            square_ref[:, lanes] = jnp.sum(full * full, axis=0, keepdims=True)
            a, b = divmod(k, count // PLANES)
            cross_refs[b][a] = dot(left_ref[:R, :], low).astype(LOW)

    return kernel(
        body,
        [
            ((rows_padded, total), LOW),
            ((R, total), LOW),
            ((1, total), F32),
            ((1, total), F32),
        ]
        + [((PLANES, R, width), LOW)] * (count // PLANES),
        weight,
        left_pair,
        right,
        magnitude,
        scalars=scalars,
    )


def inner_product(inputs, lefts_pair):
    half = lefts_pair.shape[0] // 2
    return dot(inputs, lefts_pair[:half], 1, 1) + dot(inputs, lefts_pair[half:], 1, 1)


def adapter_term(inner, rights_pair):
    half = rights_pair.shape[0] // 2
    high, rest = split(inner)
    return (
        dot(high, rights_pair[:half]) + dot(rest, rights_pair[:half]) + dot(high, rights_pair[half:])
    )


def halves_turned(values):
    return pltpu.roll(values, HD // 2, axis=1)


def allowed_pairs(seg_rows, seg_cols):
    length = seg_rows.shape[0]
    row_at = lax.broadcasted_iota(jnp.int32, (length, length), 0)
    col_at = lax.broadcasted_iota(jnp.int32, (length, length), 1)
    return (seg_rows == seg_cols) & (col_at <= row_at)


def lane_sums_as_row(values):
    folded = values[:, :128]
    for at in range(128, values.shape[1], 128):
        folded = folded + values[:, at : at + 128]
    return jnp.sum(folded.T, axis=0, keepdims=True)


def row_as_columns(row, lanes):
    return jnp.broadcast_to(row, (lanes, row.shape[1])).T


def put_chunks(refs, values, width):
    for k, ref in enumerate(refs):
        ref[...] = values[:, k * width : (k + 1) * width].astype(LOW)


def first_half_body(*refs):
    count = (len(refs) - 20) // 2
    chunk_refs = refs[:count]
    (
        weight_ref,
        square_ref,
        magnitude_ref,
        left_ref,
        right_ref,
        cos_ref,
        sin_ref,
        segr_ref,
        segc_ref,
        out_full_ref,
    ) = refs[count : count + 10]
    (
        normed_ref,
        proj_ref,
        inner_ref,
        q_ref,
        k_ref,
        v_ref,
        mix_ref,
        lse_ref,
        inverse_ref,
        factor_ref,
    ) = refs[count + 10 : count + 20]
    part_refs = refs[count + 20 :]
    tokens, width = mix_ref.shape
    heads = width // HD
    gain_at = chunk_refs[0].shape[0] - 16
    squares = jnp.zeros((tokens, width), F32)
    for ref in chunk_refs:
        values = ref[:tokens, :].astype(F32)
        squares = squares + values * values
    inverse = lax.rsqrt(jnp.sum(squares, axis=1, keepdims=True) / (width * count) + EPS)
    inverse_ref[...] = inverse
    for k, ref in enumerate(chunk_refs):
        gain = ref[gain_at : gain_at + 16, :].astype(F32)[:1]
        values = ref[:tokens, :].astype(F32)
        normed_ref[:, k * width : (k + 1) * width] = (values * inverse * gain).astype(LOW)
    normed = normed_ref[...]
    inner = inner_product(normed, left_ref[...])
    inner_ref[...] = inner
    proj_ref[...] = dot(normed, weight_ref[...]) + adapter_term(inner, right_ref[...])
    factor_ref[...] = magnitude_ref[...] / jnp.sqrt(square_ref[...])
    cosine = cos_ref[...]
    sine = sin_ref[...]
    allowed = allowed_pairs(segr_ref[...], segc_ref[...])
    for head in range(heads):
        at = head * HD
        taken = []
        for member in range(3):
            lanes = slice(member * width + at, member * width + at + HD)
            taken.append(proj_ref[:, lanes] * factor_ref[:, lanes])
        queries = (taken[0] * cosine + halves_turned(taken[0]) * sine).astype(LOW)
        keys = (taken[1] * cosine + halves_turned(taken[1]) * sine).astype(LOW)
        values = taken[2].astype(LOW)
        logits = jnp.where(allowed, dot(queries, keys, 1, 1) * HD ** (-0.5), NEGATIVE)
        highest = jnp.max(logits, axis=1, keepdims=True)
        powers = jnp.exp(logits - highest)
        totals = jnp.sum(powers, axis=1, keepdims=True)
        probs_low = (powers / totals).astype(LOW)
        mix_ref[:, at : at + HD] = dot(probs_low, values).astype(LOW)
        q_ref[:, at : at + HD] = queries
        k_ref[:, at : at + HD] = keys
        v_ref[:, at : at + HD] = values
        lse_ref[:, head : head + 1] = highest + jnp.log(totals)
    put_chunks(part_refs, dot(mix_ref[...], out_full_ref[...]), width)


def feed_forward_body(*refs):
    count = (len(refs) - 11) // 2
    chunk_refs = refs[:count]
    (
        gain_ref,
        full_ref,
        square_ref,
        magnitude_ref,
        dact_ref,
    ) = refs[count : count + 5]
    scaled_ref, inverse_ref, act_ref, low_ref, scale_ref, token_ref = refs[count + 5 : count + 11]
    part_refs = refs[count + 11 :]
    width = chunk_refs[0].shape[1]
    hidden = act_ref.shape[1]
    squares = jnp.zeros(chunk_refs[0].shape, F32)
    for k, ref in enumerate(chunk_refs):
        lanes = slice(k * width, (k + 1) * width)
        values = ref[...]
        scaled_ref[:, lanes] = values
        raw = values.astype(F32) * (1.0 / gain_ref[:, lanes])
        squares = squares + raw * raw
    inverse = lax.rsqrt(jnp.sum(squares, axis=1, keepdims=True) / (width * count) + EPS)
    inverse_ref[...] = inverse
    proj = dot(scaled_ref[...], full_ref[...])
    factor = magnitude_ref[...] / jnp.sqrt(jnp.where(square_ref[...] == 0.0, 1.0, square_ref[...]))
    gate_factor, up_factor = factor[:, :hidden], factor[:, hidden:]
    gate_proj, up_proj = proj[:, :hidden], proj[:, hidden:]
    gate_shaped = gate_proj * inverse
    up_shaped = up_proj * inverse
    gate = gate_shaped * gate_factor
    upper = up_shaped * up_factor
    sigma = 1.0 / (1.0 + jnp.exp(-gate))
    silu = gate * sigma
    act_ref[...] = (silu * upper).astype(LOW)
    grads = dact_ref[...]
    grad_gate = grads * upper * (sigma * (1.0 + gate * (1.0 - sigma)))
    grad_up = grads * silu

    @pl.when(pl.program_id(0) == 0)
    def _():
        scale_ref[...] = jnp.zeros_like(scale_ref)

    scale_ref[:, :hidden] += jnp.sum(grad_gate * gate_shaped, axis=0, keepdims=True)
    scale_ref[:, hidden:] += jnp.sum(grad_up * up_shaped, axis=0, keepdims=True)
    low_gate = (grad_gate * gate_factor).astype(LOW)
    low_up = (grad_up * up_factor).astype(LOW)
    low_ref[:, :hidden] = low_gate
    low_ref[:, hidden:] = low_up
    token_ref[...] = lane_sums_as_row(
        low_gate.astype(F32) * gate_proj + low_up.astype(F32) * up_proj
    )
    for k, ref in enumerate(part_refs):
        ref[...] = dot(low_ref[...], full_ref[k * width : (k + 1) * width, :], 1, 1).astype(LOW)


def down_body(act_ref, full_ref, *part_refs):
    put_chunks(part_refs, dot(act_ref[...], full_ref[...]), part_refs[0].shape[1])


def down_grad_body(*refs):
    chunk_refs = refs[:-6]
    square_ref, magnitude_ref, full_ref, left_ref, grad_ref, dact_ref = refs[-6:]
    width = chunk_refs[0].shape[1]
    tokens = grad_ref.shape[0]
    factor = magnitude_ref[...] / jnp.sqrt(square_ref[...])
    for k, ref in enumerate(chunk_refs):
        lanes = slice(k * width, (k + 1) * width)
        grad_ref[:, lanes] = (ref[:tokens, :].astype(F32) * factor[:, lanes]).astype(LOW)
        left_ref[:, lanes] = ref[tokens:, :]
    dact_ref[...] = dot(grad_ref[...], full_ref[...], 1, 1)


def middle_body(*refs):
    piece_refs = refs[:-6]
    token_ref, gain_ref, factor_ref, shaped_ref, middle_ref, chunk_ref = refs[-6:]
    shaped = summed(piece_refs)
    shaped_ref[...] = shaped
    middle = token_ref[...].astype(F32) + shaped * factor_ref[...]
    middle_ref[...] = middle
    chunk_ref[...] = (middle * gain_ref[...]).astype(LOW)


def result_body(*refs):
    piece_refs = refs[:-5]
    middle_ref, cotangent_ref, factor_ref, out_ref, scale_ref = refs[-5:]
    shaped = summed(piece_refs)
    out_ref[...] = (middle_ref[...] + shaped * factor_ref[...]).astype(LOW)
    scale_ref[...] = jnp.sum(cotangent_ref[...].astype(F32) * shaped, axis=0, keepdims=True)


def grad_middle_body(*refs):
    piece_refs = refs[:-10]
    (
        cotangent_ref,
        middle_ref,
        inverse_ref,
        gain_ref,
        token_ref,
        factor_ref,
        shaped_ref,
        grad_ref,
        low_ref,
        scale_ref,
    ) = refs[-10:]
    _, width = middle_ref.shape
    inverse = inverse_ref[...]
    token_sums = row_as_columns(token_ref[...], width)
    model_width = width * lax.axis_size("mp")
    grads = (
        cotangent_ref[...].astype(F32)
        + inverse * gain_ref[...] * summed(piece_refs)
        - middle_ref[...] * (inverse * inverse * inverse / model_width * token_sums)
    )
    grad_ref[...] = grads
    low_ref[...] = (grads * factor_ref[...]).astype(LOW)
    scale_ref[...] = jnp.sum(grads * shaped_ref[...], axis=0, keepdims=True)


def input_grad_body(*refs):
    piece_refs = refs[:-6]
    grad_ref, token_ref, inverse_ref, gain_ref, sum_ref, out_ref = refs[-6:]
    _, width = grad_ref.shape
    inverse = inverse_ref[...]
    token_sums = row_as_columns(sum_ref[...], width)
    model_width = width * lax.axis_size("mp")
    out_ref[...] = (
        grad_ref[...]
        + inverse * gain_ref[...] * summed(piece_refs)
        - token_ref[...].astype(F32) * (inverse * inverse / model_width * token_sums)
    )


def second_half_body(*refs):
    count = (len(refs) - 16) // 2
    chunk_refs = refs[:count]
    (
        out_full_ref,
        q_ref,
        k_ref,
        v_ref,
        lse_ref,
        proj_ref,
        factor_ref,
        cos_ref,
        sin_ref,
        segr_ref,
        segc_ref,
        full_ref,
    ) = refs[count : count + 12]
    all_ref, g_ref, scale_ref, token_ref = refs[count + 12 : count + 16]
    part_refs = refs[count + 16 :]
    tokens, width = chunk_refs[0].shape
    heads = width // HD
    for k, ref in enumerate(chunk_refs):
        all_ref[:, k * width : (k + 1) * width] = ref[...]
    mixed_grads = dot(all_ref[...], out_full_ref[...], 1, 1).astype(LOW)
    cosine = cos_ref[...]
    sine = sin_ref[...]
    allowed = allowed_pairs(segr_ref[...], segc_ref[...])
    token_total = jnp.zeros((tokens, HD), F32)
    for head in range(heads):
        at = head * HD
        queries = q_ref[:, at : at + HD]
        keys = k_ref[:, at : at + HD]
        values = v_ref[:, at : at + HD]
        mixed_grad = mixed_grads[:, at : at + HD]
        logits = jnp.where(allowed, dot(queries, keys, 1, 1) * HD ** (-0.5), NEGATIVE)
        probs = jnp.exp(logits - lse_ref[:, head : head + 1])
        prob_grad = dot(mixed_grad, values, 1, 1)
        delta = jnp.sum(prob_grad * probs, axis=1, keepdims=True)
        raw_grad = (probs * (prob_grad - delta) * HD ** (-0.5)).astype(LOW)
        query_grad = dot(raw_grad, keys)
        key_grad = dot(raw_grad, queries, 0, 0)
        value_grad = dot(probs.astype(LOW), mixed_grad, 0, 0)
        grads = (
            query_grad * cosine - halves_turned(query_grad) * sine,
            key_grad * cosine - halves_turned(key_grad) * sine,
            value_grad,
        )
        for member in range(3):
            lanes = slice(member * width + at, member * width + at + HD)
            shaped = proj_ref[:, lanes]
            lowered = (grads[member] * factor_ref[:, lanes]).astype(LOW)
            g_ref[:, lanes] = lowered
            scale_ref[:, lanes] = jnp.sum(grads[member] * shaped, axis=0, keepdims=True)
            token_total = token_total + lowered.astype(F32) * shaped
    token_ref[...] = lane_sums_as_row(token_total)
    for k, ref in enumerate(part_refs):
        ref[...] = dot(g_ref[...], full_ref[k * width : (k + 1) * width, :], 1, 1).astype(LOW)


def put_bundles(refs, rows, values):
    inner = len(refs)
    width = refs[0].shape[2]
    for b, ref in enumerate(refs):
        for a in range(PLANES):
            at = (a * inner + b) * width
            ref[a, rows, :] = values[:, at : at + width].astype(LOW)


def negative_ratio(scale, magnitude, square):
    norm = jnp.sqrt(jnp.where(square == 0.0, 1.0, square))
    return -scale * magnitude / (norm * norm * norm)


def column_adapters(
    low_grad, inputs, inner, inverse, full, square, magnitude, scale, lefts, rights, members
):
    half = rights.shape[0] // 2
    high = rights[:half]
    ratio = negative_ratio(scale, magnitude, square)
    rank = dot(low_grad, high, 1, 1)
    if inverse is not None:
        rank = rank * inverse
        inner = inner * inverse
    left_part = dot(rank.astype(LOW), inputs, 0, 0) + dot(
        (high.astype(F32) * ratio).astype(LOW), full, 1, 1
    )
    right_part = dot(inner.astype(LOW), low_grad, 0, 0) + ratio * dot(lefts[:half], full)
    size = low_grad.shape[1] // members
    rights_out = [
        right_part[slot * R : (slot + 1) * R, slot * size : (slot + 1) * size]
        for slot in range(members)
    ]
    return SCALE * left_part, rights_out


def two_adapters_body(
    low_ref,
    scaled_ref,
    inverse_ref,
    full_ref,
    square_ref,
    magnitude_ref,
    scale_ref,
    left_ref,
    right_ref,
    broad_ref,
    *bundle_refs,
):
    hidden = broad_ref.shape[1]
    left_part, rights_out = column_adapters(
        low_ref[...],
        scaled_ref[...],
        inner_product(scaled_ref[...], left_ref[...]),
        inverse_ref[...],
        full_ref[...],
        square_ref[...],
        magnitude_ref[...],
        scale_ref[...],
        left_ref[...],
        right_ref[...],
        2,
    )
    put_bundles(bundle_refs, slice(None), left_part)
    broad_ref[:R, :] = rights_out[0]
    broad_ref[R : 2 * R, :] = rights_out[1]
    broad_ref[2 * R : 2 * R + 1, :] = scale_ref[:, :hidden]
    broad_ref[2 * R + 1 : 2 * R + 2, :] = scale_ref[:, hidden:]
    broad_ref[2 * R + 2 :, :] = jnp.zeros((6, hidden), F32)


def row_adapters(grads, inputs, high, left_rows):
    rank = dot(grads, high, 1, 1)
    left_part = SCALE * dot(rank.astype(LOW), inputs, 0, 0)
    inner = dot(inputs, left_rows, 1, 1)
    return left_part, dot(inner.astype(LOW), grads, 0, 0)


def ratio_adapters_body(
    out_high_ref, out_full_ref, down_high_ref, down_full_ref, ratio_ref, rows_ref
):
    width = rows_ref.shape[1]
    for slot, (high_ref, full_ref) in enumerate(
        ((out_high_ref, out_full_ref), (down_high_ref, down_full_ref))
    ):
        scaled = (high_ref[...].astype(F32) * ratio_ref[slot : slot + 1, :]).astype(LOW)
        part = SCALE * dot(scaled, full_ref[...], 1, 1)
        for first in range(0, part.shape[1], width):
            at = slot * R + first // width * R
            rows_ref[at : at + R, :] = part[:, first : first + width]


def end_adapters_body(*refs):
    (
        low_ref,
        normed_ref,
        inner_ref,
        full_ref,
        square_ref,
        magnitude_ref,
        scale_ref,
        left_ref,
        right_ref,
        gout_ref,
        mixed_ref,
        out_high_ref,
        out_left_ref,
        gdown_ref,
        act_ref,
        down_high_ref,
        down_left_ref,
    ) = refs[:17]
    inner = (len(refs) - 18) // 4
    moved_refs, rows_ref, bundle_refs = refs[17:-inner - 1], refs[-inner - 1], refs[-inner:]
    for b, ref in enumerate(bundle_refs):
        ref[:, 5 * R : 7 * R, :] = moved_refs[b][...]
        ref[:, 7 * R : 8 * R, :] = moved_refs[inner + b][...]
        ref[:, 8 * R :, :] = moved_refs[2 * inner + b][...]
    width = rows_ref.shape[1]
    left_part, rights_out = column_adapters(
        low_ref[...],
        normed_ref[...],
        inner_ref[...],
        None,
        full_ref[...],
        square_ref[...],
        magnitude_ref[...],
        scale_ref[...],
        left_ref[...],
        right_ref[...],
        3,
    )
    put_bundles(bundle_refs, slice(0, 3 * R), left_part)
    left_out, right_out = row_adapters(
        gout_ref[...],
        mixed_ref[...],
        out_high_ref[...],
        out_left_ref[:R, :],
    )
    put_bundles(bundle_refs, slice(3 * R, 4 * R), right_out)
    left_down, right_down = row_adapters(
        gdown_ref[...],
        act_ref[...],
        down_high_ref[...],
        down_left_ref[:R, :],
    )
    put_bundles(bundle_refs, slice(4 * R, 5 * R), right_down)
    at = 0
    for values in rights_out + [left_out]:
        rows_ref[at : at + R, :] = values
        at += R
    for first in range(0, left_down.shape[1], width):
        rows_ref[at : at + R, :] = left_down[:, first : first + width]
        at += R
    for slot in range(3):
        rows_ref[at + slot : at + slot + 1, :] = scale_ref[:, slot * width : (slot + 1) * width]
    rows_ref[at + 3 : at + 8, :] = jnp.zeros((5, width), F32)


def statistics_body(*refs):
    out_ref = refs[-1]
    rows = lax.broadcasted_iota(jnp.int32, out_ref.shape, 0)
    lanes = lax.broadcasted_iota(jnp.int32, out_ref.shape, 1)
    table = jnp.zeros(out_ref.shape, F32)
    member = 0
    for slot, members in enumerate((3, 1, 2, 1)):
        norms = jnp.sqrt(refs[2 * slot][...])
        drifts = refs[2 * slot + 1][...] - norms
        size = norms.shape[1] // members
        for part in range(members):
            taken = slice(part * size, (part + 1) * size)
            norm, drift = norms[:, taken], drifts[:, taken]
            first = jnp.sum(drift * drift, axis=1, keepdims=True)
            second = jnp.sum(norm, axis=1, keepdims=True)
            table = jnp.where(rows == member, jnp.where(lanes == 0, first, second), table)
            member += 1
    out_ref[...] = table


def on_device(
    tokens,
    cotangent,
    segment_ids,
    attention_gain,
    feedforward_gain,
    *parameters,
):
    count = lax.axis_size("mp")
    inner_count = count // PLANES
    place = lax.axis_index("mp")
    scalars = jnp.stack([place, lax.axis_index("dp")]).astype(jnp.int32)
    weights = parameters[:7]
    lefts = parameters[7::3]
    rights = parameters[8::3]
    magnitudes = parameters[9::3]
    token_count, width = tokens.shape
    hidden = weights[4].shape[1] // count
    hidden_padded = round_up(hidden)
    widths = [weight.shape[1] // count for weight in weights]
    chunk_shape = (token_count, width)
    rights_one, rights_two, magnitude_one, magnitude_two, magnitude_out, magnitude_down = (
        own_factors(rights, magnitudes, width, hidden, hidden_padded, scalars)
    )

    def lefts_of(members):
        return split_rows(
            SCALE * jnp.concatenate([lefts[member].T for member in members], axis=0)
        )

    own_one, *blocks_one = cut_blocks(weights[:3], width, width, scalars)
    extended = jnp.concatenate(
        [
            tokens,
            lefts_of((0, 1, 2)),
            attention_gain[None],
            feedforward_gain[None],
            jnp.zeros((14, width), LOW),
        ],
        axis=0,
    )
    token_chunks = gather(extended)
    pieces_one = exchanged(blocks_one)
    lefts_one, gain_two_all = gathered_lefts(token_chunks, token_count)
    weight_one, full_one, squares_one = assemble(
        own_one, pieces_one, lefts_one, rights_one, scalars, True
    )

    length = segment_ids.shape[1]
    key_index = jnp.arange(length, dtype=jnp.int32)
    segments = segment_ids[0]
    change = jnp.concatenate(
        [jnp.ones((1,), jnp.int32), (segments[1:] != segments[:-1]).astype(jnp.int32)]
    )
    places = (key_index - lax.cummax(key_index * change, axis=0)).astype(F32)
    half = HD // 2
    freqs = THETA ** (-2.0 * jnp.arange(half, dtype=F32) / HD)
    angles = places[:, None] * freqs[None, :]
    cosine = jnp.cos(angles)
    sine = jnp.sin(angles)
    cosine = jnp.concatenate([cosine, cosine], axis=1)
    sine = jnp.concatenate([-sine, sine], axis=1)
    seg_rows = segments[:, None]
    seg_cols = segments[None, :]

    left_out = lefts_of((3,))
    left_down = pad_to(lefts_of((6,)), hidden_padded, 1)
    full_out, high_out, squares_out, _, *cross_out = row_block(
        weights[3], left_out, rights[3], magnitudes[3][None], width, width, scalars
    )
    full_down, high_down, squares_down, magnitude_down_all, *cross_down = row_block(
        weights[6], left_down, rights[6], magnitudes[6][None], width, hidden_padded, scalars
    )
    squares_all = total_relative(
        jnp.concatenate([squares_out, squares_down], axis=0)
        .reshape(2, count, width)
        .transpose(1, 0, 2),
    )
    square_out, square_down = squares_all[0, :1], squares_all[0, 1:]
    square_down_all = squares_all[:, 1].reshape(1, count * width)
    factor_out = magnitude_out / jnp.sqrt(square_out)
    factor_down = magnitude_down / jnp.sqrt(square_down)

    heads = width // HD
    (
        normed_one,
        proj_one,
        inner_one,
        queries,
        keys,
        values,
        mixed,
        log_totals,
        inverse_one,
        factor_one,
        *parts_out,
    ) = kernel(
        first_half_body,
        [
            ((token_count, count * width), LOW),
            ((token_count, 3 * width), F32),
            ((token_count, 3 * R), F32),
        ]
        + [(chunk_shape, LOW)] * 4
        + [((token_count, heads), F32), ((token_count, 1), F32), ((1, 3 * width), F32)]
        + [(chunk_shape, LOW)] * count,
        *token_chunks,
        weight_one,
        squares_one,
        magnitude_one,
        lefts_one,
        rights_one,
        cosine,
        sine,
        seg_rows,
        seg_cols,
        full_out,
    )
    gain_one = attention_gain.astype(F32)[None]
    gain_two = feedforward_gain.astype(F32)[None]
    shaped_out, middle, chunk_two = kernel(
        middle_body,
        [(chunk_shape, F32), (chunk_shape, F32), (chunk_shape, LOW)],
        *scatter_pieces(parts_out),
        tokens,
        gain_two,
        factor_out,
    )

    cotangent_chunks = gather(jnp.concatenate([cotangent, lefts_of((4, 5))], axis=0))
    lefts_two, grad_down_all, grad_activated = kernel(
        down_grad_body,
        [
            ((4 * R, count * width), LOW),
            ((token_count, count * width), LOW),
            ((token_count, hidden_padded), F32),
        ],
        *cotangent_chunks,
        square_down_all,
        magnitude_down_all,
        full_down,
    )
    own_two, *blocks_two = cut_blocks(weights[4:6], hidden, hidden_padded, scalars)
    full_two, squares_two = assemble(
        own_two, exchanged(blocks_two), lefts_two, rights_two, scalars, False
    )

    scaled_two, inverse_two, activated, low_two, scale_two, token_two, *parts_two = by_rows(
        feed_forward_body,
        2,
        count,
        (count + 4,),
        (4,),
        5,
        [
            ((token_count, count * width), LOW),
            ((token_count, 1), F32),
            ((token_count, hidden_padded), LOW),
            ((token_count, 2 * hidden_padded), LOW),
            ((1, 2 * hidden_padded), F32),
            ((1, token_count), F32),
        ]
        + [(chunk_shape, LOW)] * count,
        *gather(chunk_two),
        gain_two_all,
        full_two,
        squares_two,
        magnitude_two,
        grad_activated,
    )
    token_two = total_over(token_two, "mp")
    grad_middle, grad_out, scale_out = kernel(
        grad_middle_body,
        [(chunk_shape, F32), (chunk_shape, LOW), ((1, width), F32)],
        *scatter_pieces(parts_two),
        cotangent,
        middle,
        inverse_two,
        gain_two,
        token_two,
        factor_out,
        shaped_out,
    )
    parts_down = by_rows(
        down_body, 2, 1, (), (), None, [(chunk_shape, LOW)] * count, activated, full_down
    )
    layer_out, scale_down = kernel(
        result_body,
        [(chunk_shape, LOW), ((1, width), F32)],
        *scatter_pieces(parts_down),
        middle,
        cotangent,
        factor_down,
    )

    grad_out_all, low_one, scale_one, token_one, *parts_one = kernel(
        second_half_body,
        [
            ((token_count, count * width), LOW),
            ((token_count, 3 * width), LOW),
            ((1, 3 * width), F32),
            ((1, token_count), F32),
        ]
        + [(chunk_shape, LOW)] * count,
        *gather(grad_out),
        full_out,
        queries,
        keys,
        values,
        log_totals,
        proj_one,
        factor_one,
        cosine,
        sine,
        seg_rows,
        seg_cols,
        full_one,
    )
    token_one = total_over(token_one, "mp")
    (input_gradient,) = kernel(
        input_grad_body,
        [(chunk_shape, F32)],
        *scatter_pieces(parts_one),
        grad_middle,
        tokens,
        inverse_one,
        gain_one,
        token_one,
    )

    broad, *bundles = kernel(
        two_adapters_body,
        [((2 * R + 8, hidden_padded), F32)] + [((PLANES, 2 * R, width), LOW)] * inner_count,
        low_two,
        scaled_two,
        inverse_two,
        full_two,
        squares_two,
        magnitude_two,
        scale_two,
        lefts_two,
        rights_two,
    )
    broad = total_over(broad, "dp")

    ratio_rows = small_gather(
        jnp.concatenate(
            [
                negative_ratio(scale_out, magnitude_out, square_out),
                negative_ratio(scale_down, magnitude_down, square_down),
            ],
            axis=0,
        ),
    )
    slabs = hidden_padded // width
    rows_end, *bundles_end = kernel(
        end_adapters_body,
        [(((4 + slabs) * R + 8, width), F32)] + [((PLANES, 9 * R, width), LOW)] * inner_count,
        low_one,
        normed_one,
        inner_one,
        full_one,
        squares_one,
        magnitude_one,
        scale_one,
        lefts_one,
        rights_one,
        grad_out_all,
        mixed,
        high_out,
        left_out,
        grad_down_all,
        activated,
        high_down,
        left_down,
        *bundles,
        *cross_out,
        *cross_down,
    )
    spread = small_scatter(bundles_end)
    crossed = spread[7 * R :]
    (rows_ratio,) = kernel(
        ratio_adapters_body,
        [(((1 + slabs) * R, width), F32)],
        high_out,
        full_out,
        high_down,
        full_down,
        ratio_rows,
    )
    last = total_over(
        jnp.concatenate(
            [
                spread[: 7 * R],
                rows_end[: 3 * R],
                rows_end[3 * R : (4 + slabs) * R] + rows_ratio,
                rows_end[(4 + slabs) * R :][:3],
                scale_out,
                scale_down,
                jnp.zeros((3, width), F32),
            ],
            axis=0,
        ),
        "dp",
    )

    own_square = [squares_one[:, slot * width : (slot + 1) * width] for slot in range(3)] + [
        square_out,
        squares_two[:, :hidden_padded],
        squares_two[:, hidden_padded:],
        square_down,
    ]
    (stat_sums,) = kernel(
        statistics_body,
        [((8, 128), F32)],
        squares_one,
        magnitude_one,
        square_out,
        magnitude_out,
        squares_two,
        magnitude_two,
        square_down,
        magnitude_down,
    )
    stat_sums = total_over(stat_sums, "mp")[:7, :2]
    columns_all = jnp.array([weight.shape[1] for weight in weights], F32)[:, None]
    means = stat_sums / columns_all
    statistics = jnp.concatenate([jnp.sqrt(means[:, :1]), means[:, 1:]], axis=1)

    def rows_of(values, slot):
        return values[slot * R : (slot + 1) * R]

    scales_at = (11 + slabs) * R
    right_ends = [
        rows_of(last, 3 + slot)
        + negative_ratio(last[scales_at + 3 + slot][None], magnitude, square)
        * rows_of(crossed, slot)
        for slot, magnitude, square in (
            (0, magnitude_out, square_out),
            (1, magnitude_down, square_down),
        )
    ]
    down_rows = jnp.concatenate([rows_of(last, 11 + slab) for slab in range(slabs)], axis=1)
    left_grads = [rows_of(last, slot).T for slot in range(3)] + [
        rows_of(last, 10).T,
        rows_of(last, 5).T,
        rows_of(last, 6).T,
        down_rows[:, :hidden].T,
    ]
    right_grads = [rows_of(last, 7 + slot) for slot in range(3)] + [
        right_ends[0],
        rows_of(broad, 0)[:, :hidden],
        rows_of(broad, 1)[:, :hidden],
        right_ends[1],
    ]
    scale_grads = [last[scales_at + slot] for slot in range(4)] + [
        broad[2 * R, :hidden],
        broad[2 * R + 1, :hidden],
        last[scales_at + 4],
    ]
    results = [layer_out, input_gradient]
    for member in range(7):
        results += [
            left_grads[member],
            right_grads[member],
            scale_grads[member] / jnp.sqrt(own_square[member][0, : widths[member]]),
        ]
    return tuple(results + [statistics])


def solution(mesh):
    grid = P("dp", "mp")
    rows = P("mp", None)
    placed = (grid, grid, P("dp", None), P("mp"), P("mp")) + (rows,) * 7 + (rows, P(), P()) * 7
    adapters = (rows, P(None, "mp"), P("mp")) * 7
    return jax.shard_map(
        on_device,
        mesh=mesh,
        in_specs=placed,
        out_specs=(grid, grid) + adapters + (P(),),
        check_vma=False,
    )
```

```python
import jax
import jax.numpy as jnp
from jax import lax
from jax.experimental import pallas as pl
from jax.experimental.pallas import tpu as pltpu
from jax.sharding import PartitionSpec as P

HD = 128
R = 16
ALPHA = 32
SCALE = ALPHA / R
EPS = 1e-05
THETA = 10000.0
NEGATIVE = -1e30
PLANES = 4
CORES = 2
LOW = jnp.bfloat16
F32 = jnp.float32


def swap(values, offset, axis):
    count = lax.axis_size(axis)
    return lax.ppermute(values, axis, [(place, place ^ offset) for place in range(count)])


def gather(chunk):
    count = lax.axis_size("mp")
    inner = count // PLANES
    got = [None] * count
    got[0] = chunk
    for a in range(1, PLANES):
        got[a * inner] = swap(chunk, a * inner, "mp")
    for a in range(PLANES):
        for b in range(1, inner):
            got[a * inner + b] = swap(got[a * inner], b, "mp")
    return got


def total_over(values, axis):
    offset = 1
    while offset < lax.axis_size(axis):
        values = values + swap(values, offset, axis)
        offset *= 2
    return values


def small_scatter(bundles):
    inner = len(bundles)
    held = bundles[0].astype(F32)
    for b in range(1, inner):
        held = held + swap(bundles[b], b, "mp").astype(F32)
    final = held[0]
    for a in range(1, PLANES):
        sent = held[a].astype(LOW)
        final = final + swap(sent, a * inner, "mp").astype(F32)
    return final


def total_relative(values, same):
    count = values.shape[0]
    offset = 1
    while offset < count:
        turned = [values[k ^ offset][None] for k in range(count)]
        got = swap(jnp.concatenate(turned + [same]), offset, "mp")
        values, same = values + got[:count], same + got[count:]
        offset *= 2
    return values, same


def dot(left_part, right_part, left_dim=1, right_dim=0):
    return lax.dot_general(
        left_part,
        right_part,
        (((left_dim,), (right_dim,)), ((), ())),
        preferred_element_type=F32,
    )


def split(values):
    high = values.astype(LOW)
    return high, (values - high.astype(F32)).astype(LOW)


def split_rows(values):
    high = lax.reduce_precision(values, 8, 7)
    return jnp.concatenate([high, values - high], axis=0).astype(LOW)


def round_up(size):
    return -(-size // 128) * 128


def pad_to(values, size, axis):
    if values.shape[axis] == size:
        return values
    widths = [(0, 0)] * values.ndim
    widths[axis] = (0, size - values.shape[axis])
    return jnp.pad(values, widths)


def kernel(body, outs, *operands, scalars=None, scratch=()):
    specs = [pl.BlockSpec(memory_space=pltpu.VMEM)] * len(operands)
    if scalars is not None:
        specs = [pl.BlockSpec(memory_space=pltpu.SMEM)] + specs
        operands = (scalars,) + operands
    return pl.pallas_call(
        body,
        out_shape=tuple(jax.ShapeDtypeStruct(shape, kind) for shape, kind in outs),
        in_specs=specs,
        scratch_shapes=list(scratch),
    )(*operands)


def by_rows(body, steps, chunks, rowed, summed_outs, across, outs, *operands):
    def spec(shape, by_block):
        if by_block:
            return pl.BlockSpec((shape[0] // steps, shape[1]), lambda i: (i, 0))
        return pl.BlockSpec(shape, lambda i: (0, 0))

    out_specs = [spec(shape, slot not in summed_outs) for slot, (shape, _) in enumerate(outs)]
    if across is not None:
        shape = outs[across][0]
        out_specs[across] = pl.BlockSpec((shape[0], shape[1] // steps), lambda i: (0, i))
    return pl.pallas_call(
        body,
        grid=(steps,),
        in_specs=[
            spec(operand.shape, slot < chunks or slot in rowed)
            for slot, operand in enumerate(operands)
        ],
        out_specs=out_specs,
        out_shape=[jax.ShapeDtypeStruct(shape, kind) for shape, kind in outs],
    )(*operands)


def add_low(first, *others):
    def body(*refs):
        total = refs[0][...].astype(F32)
        for ref in refs[1:-1]:
            total = total + ref[...].astype(F32)
        refs[-1][...] = total.astype(LOW)

    return kernel(body, [(first.shape, LOW)], first, *others)[0]


def scatter_pieces(parts):
    count = len(parts)
    inner = count // PLANES
    order = list(range(1, PLANES)) + [0]
    got = {a: [swap(parts[a * inner + b], b, "mp") for b in range(1, inner)] for a in order}
    sent = [swap(add_low(parts[a * inner], *got[a]), a * inner, "mp") for a in order[:-1]]
    return [parts[0]] + got[0] + sent


def summed(refs):
    total = refs[0][...].astype(F32)
    for ref in refs[1:]:
        total = total + ref[...].astype(F32)
    return total


def take_columns(ref, taken, index, width, padded):
    start = index * width
    if width % 128 == 0:
        return ref[taken, pl.ds(pl.multiple_of(start, 128), width)]
    window = round_up(width + 127)
    base = pl.multiple_of(jnp.minimum((start >> 7) << 7, ref.shape[1] - window), 128)
    values = ref[taken, pl.ds(base, window)]
    turn = lax.rem(window - (start - base), window)
    turned = pltpu.roll(values.astype(F32), turn, axis=1)[:, :padded]
    lanes = lax.broadcasted_iota(jnp.int32, turned.shape, 1)
    return jnp.where(lanes < width, turned, 0.0).astype(values.dtype)


def own_factors(rights, magnitudes, width, hidden, padded, scalars):
    def body(place_ref, *refs):
        right_refs, magnitude_refs = refs[:5], refs[5:12]
        place = place_ref[0]
        for members, size, filled, pair_ref in (
            (range(3), width, width, refs[12]),
            (range(3, 5), hidden, padded, refs[13]),
        ):
            half = len(members) * R
            pair_ref[...] = jnp.zeros_like(pair_ref)
            for slot, member in enumerate(members):
                high, rest = split(
                    take_columns(right_refs[member], slice(None), place, size, filled)
                )
                rows = slice(slot * R, (slot + 1) * R)
                lanes = slice(slot * filled, (slot + 1) * filled)
                pair_ref[rows, lanes] = high
                pair_ref[half + slot * R : half + (slot + 1) * R, lanes] = rest
        taken = [
            take_columns(
                ref,
                slice(None),
                place,
                hidden if member in (4, 5) else width,
                padded if member in (4, 5) else width,
            )
            for member, ref in enumerate(magnitude_refs)
        ]
        for slot in range(3):
            refs[14][:, slot * width : (slot + 1) * width] = taken[slot]
        refs[15][:, :padded] = taken[4]
        refs[15][:, padded:] = taken[5]
        refs[16][...] = taken[3]
        refs[17][...] = taken[6]

    return kernel(
        body,
        [
            ((6 * R, 3 * width), LOW),
            ((4 * R, 2 * padded), LOW),
            ((1, 3 * width), F32),
            ((1, 2 * padded), F32),
            ((1, width), F32),
            ((1, width), F32),
        ],
        *[rights[member] for member in (0, 1, 2, 4, 5)],
        *[values[None] for values in magnitudes],
        scalars=scalars,
    )


def gathered_lefts(chunks, tokens):
    width = chunks[0].shape[1]

    def body(*refs):
        one_ref, two_ref, gain_ref = refs[-3:]
        first, second = tokens + 6 * R, tokens + 8 * R
        for k, ref in enumerate(refs[:-3]):
            lanes = slice(k * width, (k + 1) * width)
            one_ref[:, lanes] = ref[tokens:first, :]
            two_ref[:, lanes] = ref[first:second, :]
            gain_ref[:, lanes] = ref[second : second + 16, :].astype(F32)[1:2]

    total = len(chunks) * width
    outs = [((6 * R, total), LOW), ((2 * R, total), LOW), ((1, total), F32)]
    return kernel(body, outs, *chunks)


def cut_blocks(weights, width, padded, scalars):
    count = lax.axis_size("mp")
    members = len(weights)
    rows, _ = weights[0].shape
    part = rows // lax.axis_size("dp")

    def body(place_ref, *refs):
        sources, own_ref, block_refs = refs[:members], refs[members], refs[members + 1 :]
        place = place_ref[0]
        mine = pl.ds(pl.multiple_of(place_ref[1] * part, part), part)

        for slot, ref in enumerate(sources):
            lanes = slice(slot * padded, (slot + 1) * padded)
            own_ref[:, lanes] = take_columns(ref, slice(None), place, width, padded)
            for k in range(1, count):
                block_refs[k - 1][:, lanes] = take_columns(
                    ref, mine, place ^ k, width, padded
                )

    wide = members * padded
    return kernel(
        body, [((rows, wide), LOW)] + [((part, wide), LOW)] * (count - 1), *weights, scalars=scalars
    )


def bundled(blocks):
    def body(*refs):
        for slot, ref in enumerate(refs[:-1]):
            refs[-1][slot] = ref[...]

    shape = (len(blocks),) + blocks[0].shape
    return kernel(body, [(shape, LOW)], *blocks)[0]


def exchanged(blocks):
    bundle = bundled([swap(block, k + 1, "mp") for k, block in enumerate(blocks)])
    pieces = []
    for j in range(0, lax.axis_size("dp"), CORES):
        held = bundle if j == 0 else swap(bundle, j, "dp")
        pieces.append(held)
        pieces += [swap(held, c, "dp") for c in range(1, CORES)]
    return pieces


def thrice(pair, swapped):
    half = pair.shape[0] // 2
    high, rest = pair[:half], pair[half:]
    return jnp.concatenate([high, high, rest] if swapped else [high, rest, high], axis=0)


def fold_factors(lefts, rights_pair):
    if lefts.shape[0] == rights_pair.shape[0]:
        return thrice(lefts, False), thrice(rights_pair, True)
    return jnp.concatenate([lefts, lefts], axis=0), rights_pair


def assemble(own, pieces, lefts_all, rights_pair, scalars, keep):
    count = lax.axis_size("mp")
    rows, wide = own.shape
    part = pieces[0].shape[1]
    copies = len(pieces)

    def body(place_ref, own_ref, left_ref, right_ref, *refs):
        piece_refs, (weight_ref, full_ref, square_ref) = refs[:copies], refs[copies:]
        k = pl.program_id(0)

        @pl.when(k == 0)
        def _():
            weight_ref[...] = own_ref[...]
            square_ref[...] = jnp.zeros_like(square_ref)

        @pl.when(k > 0)
        def _():
            for j, ref in enumerate(piece_refs):
                at = pl.multiple_of((place_ref[1] ^ j) * part, part)
                weight_ref[pl.ds(at, part), :] = ref[0]

        full = weight_ref[...].astype(F32) + dot(
            *fold_factors(left_ref[...], right_ref[...]), 0, 0
        )
        full_ref[...] = full.astype(LOW)
        square_ref[...] += jnp.sum(full * full, axis=0, keepdims=True)

    whole = lambda k: (0, 0)

    def body_alone(*refs):
        body(*refs[: 4 + copies], refs[-1], *refs[4 + copies : -1])

    return pl.pallas_call(
        body if keep else body_alone,
        scratch_shapes=[] if keep else [pltpu.VMEM((rows, wide), LOW)],
        grid=(count,),
        in_specs=[
            pl.BlockSpec(memory_space=pltpu.SMEM),
            pl.BlockSpec((rows, wide), whole),
            pl.BlockSpec((lefts_all.shape[0], rows), lambda k: (0, k)),
            pl.BlockSpec(rights_pair.shape, whole),
        ]
        + [pl.BlockSpec((1, part, wide), lambda k: (jnp.maximum(k - 1, 0), 0, 0))] * len(pieces),
        out_specs=[pl.BlockSpec((rows, wide), lambda k: (k, 0))] * (2 if keep else 1)
        + [pl.BlockSpec((1, wide), whole)],
        out_shape=[jax.ShapeDtypeStruct((count * rows, wide), LOW)] * (2 if keep else 1)
        + [jax.ShapeDtypeStruct((1, wide), F32)],
    )(scalars, own, lefts_all, rights_pair, *pieces)


def row_block(weight, left_pair, right, magnitude, width, rows_padded, scalars):
    count = lax.axis_size("mp")
    rows, total = weight.shape

    def body(
        place_ref,
        weight_ref,
        left_ref,
        right_ref,
        magnitude_ref,
        full_ref,
        high_ref,
        square_ref,
        moved_ref,
        *cross_refs,
    ):
        inner = count // PLANES
        lefts = thrice(left_ref[...], False)

        def one_plane(a, carry):
            for b in range(inner):
                k = a * inner + b
                at = pl.ds(pl.multiple_of((place_ref[0] ^ k) * width, width), width)
                lanes = pl.ds(pl.multiple_of(k * width, width), width)
                values = weight_ref[:, at]
                if rows < rows_padded:
                    fill = jnp.zeros((rows_padded - rows, width), LOW)
                    values = jnp.concatenate([values, fill], axis=0)
                high, rest = split(right_ref[:, at])
                pair = jnp.concatenate([high, rest], axis=0)
                high_ref[:, lanes] = high
                moved_ref[:, lanes] = magnitude_ref[:, at]
                full = values.astype(F32) + dot(lefts, thrice(pair, True), 0, 0)
                low = full.astype(LOW)
                full_ref[:, lanes] = low
                square_ref[:, lanes] = jnp.sum(full * full, axis=0, keepdims=True)
                cross_refs[b][a] = dot(left_ref[:R, :], low).astype(LOW)
            return carry

        lax.fori_loop(0, PLANES, one_plane, 0)

    return kernel(
        body,
        [
            ((rows_padded, total), LOW),
            ((R, total), LOW),
            ((1, total), F32),
            ((1, total), F32),
        ]
        + [((PLANES, R, width), LOW)] * (count // PLANES),
        weight,
        left_pair,
        right,
        magnitude,
        scalars=scalars,
    )


def adapter_term(inner, rights_pair):
    half = rights_pair.shape[0] // 2
    high, rest = split(inner)
    return (
        dot(high, rights_pair[:half]) + dot(rest, rights_pair[:half]) + dot(high, rights_pair[half:])
    )


def halves_turned(values):
    return pltpu.roll(values, HD // 2, axis=1)


def query_blocks(tokens):
    size = tokens // 2
    return [(slice(at, at + size), slice(0, at + size)) for at in range(0, tokens, size)]


def masked_logits(q_ref, k_ref, segr_ref, segc_ref, lanes, rows, seen):
    logits = dot(q_ref[rows, lanes], k_ref[seen, lanes], 1, 1) * HD ** (-0.5)
    row_at = rows.start + lax.broadcasted_iota(jnp.int32, logits.shape, 0)
    col_at = lax.broadcasted_iota(jnp.int32, logits.shape, 1)
    allowed = (segr_ref[rows, :] == segc_ref[:, seen]) & (col_at <= row_at)
    return jnp.where(allowed, logits, NEGATIVE)


def lane_sums_as_row(values):
    folded = values[:, :128]
    for at in range(128, values.shape[1], 128):
        folded = folded + values[:, at : at + 128]
    return jnp.sum(folded.T, axis=0, keepdims=True)


def row_as_columns(row, lanes):
    return jnp.broadcast_to(row, (lanes, row.shape[1])).T


def put_chunks(refs, values, width):
    for k, ref in enumerate(refs):
        ref[...] = values[:, k * width : (k + 1) * width].astype(LOW)


def first_half_body(*refs):
    count = (len(refs) - 20) // 2
    chunk_refs = refs[:count]
    (
        weight_ref,
        square_ref,
        magnitude_ref,
        left_ref,
        right_ref,
        cos_ref,
        sin_ref,
        segr_ref,
        segc_ref,
        out_full_ref,
    ) = refs[count : count + 10]
    (
        normed_ref,
        proj_ref,
        inner_ref,
        q_ref,
        k_ref,
        v_ref,
        mix_ref,
        lse_ref,
        inverse_ref,
        factor_ref,
    ) = refs[count + 10 : count + 20]
    part_refs = refs[count + 20 :]
    tokens, width = mix_ref.shape
    heads = width // HD
    gain_at = chunk_refs[0].shape[0] - 16
    squares = jnp.zeros((tokens, width), F32)
    for ref in chunk_refs:
        values = ref[:tokens, :].astype(F32)
        squares = squares + values * values
    inverse = lax.rsqrt(jnp.sum(squares, axis=1, keepdims=True) / (width * count) + EPS)
    inverse_ref[...] = inverse
    for k, ref in enumerate(chunk_refs):
        gain = ref[gain_at : gain_at + 16, :].astype(F32)[:1]
        values = ref[:tokens, :].astype(F32)
        normed_ref[:, k * width : (k + 1) * width] = (values * inverse * gain).astype(LOW)
    normed = normed_ref[...]
    half = left_ref.shape[0] // 2
    inner = dot(normed, left_ref[:half, :], 1, 1) + dot(normed, left_ref[half:, :], 1, 1)
    inner_ref[...] = inner
    proj_ref[...] = dot(normed, weight_ref[...]) + adapter_term(inner, right_ref[...])
    factor_ref[...] = magnitude_ref[...] / jnp.sqrt(square_ref[...])
    cosine = cos_ref[...]
    sine = sin_ref[...]

    def one_head(head, carry):
        lanes = [
            pl.ds(pl.multiple_of(member * width + head * HD, HD), HD) for member in range(3)
        ]
        taken = [proj_ref[:, at] * factor_ref[:, at] for at in lanes]
        at = lanes[0]
        q_ref[:, at] = (taken[0] * cosine + halves_turned(taken[0]) * sine).astype(LOW)
        k_ref[:, at] = (taken[1] * cosine + halves_turned(taken[1]) * sine).astype(LOW)
        v_ref[:, at] = taken[2].astype(LOW)
        for rows, seen in query_blocks(tokens):
            logits = masked_logits(q_ref, k_ref, segr_ref, segc_ref, at, rows, seen)
            highest = jnp.max(logits, axis=1, keepdims=True)
            powers = jnp.exp(logits - highest)
            totals = jnp.sum(powers, axis=1, keepdims=True)
            probs_low = (powers / totals).astype(LOW)
            mix_ref[rows, at] = dot(probs_low, v_ref[seen, at]).astype(LOW)
            lse_ref[head, rows, :] = highest + jnp.log(totals)
        return carry

    lax.fori_loop(0, heads, one_head, 0)
    put_chunks(part_refs, dot(mix_ref[...], out_full_ref[...]), width)


def feed_forward_body(*refs):
    count = (len(refs) - 11) // 2
    chunk_refs = refs[:count]
    (
        gain_ref,
        full_ref,
        square_ref,
        magnitude_ref,
        dact_ref,
    ) = refs[count : count + 5]
    scaled_ref, inverse_ref, act_ref, low_ref, scale_ref, token_ref = refs[count + 5 : count + 11]
    part_refs = refs[count + 11 :]
    width = chunk_refs[0].shape[1]
    hidden = act_ref.shape[1]
    squares = jnp.zeros(chunk_refs[0].shape, F32)
    for k, ref in enumerate(chunk_refs):
        lanes = slice(k * width, (k + 1) * width)
        values = ref[...]
        scaled_ref[:, lanes] = values
        raw = values.astype(F32) * (1.0 / gain_ref[:, lanes])
        squares = squares + raw * raw
    inverse = lax.rsqrt(jnp.sum(squares, axis=1, keepdims=True) / (width * count) + EPS)
    inverse_ref[...] = inverse
    proj = dot(scaled_ref[...], full_ref[...])
    factor = magnitude_ref[...] / jnp.sqrt(jnp.where(square_ref[...] == 0.0, 1.0, square_ref[...]))
    gate_factor, up_factor = factor[:, :hidden], factor[:, hidden:]
    gate_proj, up_proj = proj[:, :hidden], proj[:, hidden:]
    gate_shaped = gate_proj * inverse
    up_shaped = up_proj * inverse
    gate = gate_shaped * gate_factor
    upper = up_shaped * up_factor
    sigma = 1.0 / (1.0 + jnp.exp(-gate))
    silu = gate * sigma
    act_ref[...] = (silu * upper).astype(LOW)
    grads = dact_ref[...]
    grad_gate = grads * upper * (sigma * (1.0 + gate * (1.0 - sigma)))
    grad_up = grads * silu

    @pl.when(pl.program_id(0) == 0)
    def _():
        scale_ref[...] = jnp.zeros_like(scale_ref)

    scale_ref[:, :hidden] += jnp.sum(grad_gate * gate_shaped, axis=0, keepdims=True)
    scale_ref[:, hidden:] += jnp.sum(grad_up * up_shaped, axis=0, keepdims=True)
    low_gate = (grad_gate * gate_factor).astype(LOW)
    low_up = (grad_up * up_factor).astype(LOW)
    low_ref[:, :hidden] = low_gate
    low_ref[:, hidden:] = low_up
    token_ref[...] = lane_sums_as_row(
        low_gate.astype(F32) * gate_proj + low_up.astype(F32) * up_proj
    )
    for k, ref in enumerate(part_refs):
        ref[...] = dot(low_ref[...], full_ref[k * width : (k + 1) * width, :], 1, 1).astype(LOW)


def down_body(act_ref, full_ref, *part_refs):
    put_chunks(part_refs, dot(act_ref[...], full_ref[...]), part_refs[0].shape[1])


def down_grad_body(*refs):
    chunk_refs = refs[:-5]
    square_ref, magnitude_ref, full_ref, grad_ref, dact_ref = refs[-5:]
    width = chunk_refs[0].shape[1]
    factor = magnitude_ref[...] / jnp.sqrt(square_ref[...])
    for k, ref in enumerate(chunk_refs):
        lanes = slice(k * width, (k + 1) * width)
        grad_ref[:, lanes] = (ref[...].astype(F32) * factor[:, lanes]).astype(LOW)
    dact_ref[...] = dot(grad_ref[...], full_ref[...], 1, 1)


def middle_body(*refs):
    piece_refs = refs[:-6]
    token_ref, gain_ref, factor_ref, shaped_ref, middle_ref, chunk_ref = refs[-6:]
    shaped = summed(piece_refs)
    shaped_ref[...] = shaped
    middle = token_ref[...].astype(F32) + shaped * factor_ref[...]
    middle_ref[...] = middle
    chunk_ref[...] = (middle * gain_ref[...]).astype(LOW)


def result_body(*refs):
    piece_refs = refs[:-5]
    middle_ref, cotangent_ref, factor_ref, out_ref, scale_ref = refs[-5:]
    shaped = summed(piece_refs)
    out_ref[...] = (middle_ref[...] + shaped * factor_ref[...]).astype(LOW)
    scale_ref[...] = jnp.sum(cotangent_ref[...].astype(F32) * shaped, axis=0, keepdims=True)


def grad_middle_body(*refs):
    piece_refs = refs[:-10]
    (
        cotangent_ref,
        middle_ref,
        inverse_ref,
        gain_ref,
        token_ref,
        factor_ref,
        shaped_ref,
        grad_ref,
        low_ref,
        scale_ref,
    ) = refs[-10:]
    _, width = middle_ref.shape
    inverse = inverse_ref[...]
    token_sums = row_as_columns(token_ref[...], width)
    model_width = width * lax.axis_size("mp")
    grads = (
        cotangent_ref[...].astype(F32)
        + inverse * gain_ref[...] * summed(piece_refs)
        - middle_ref[...] * (inverse * inverse * inverse / model_width * token_sums)
    )
    grad_ref[...] = grads
    low_ref[...] = (grads * factor_ref[...]).astype(LOW)
    scale_ref[...] = jnp.sum(grads * shaped_ref[...], axis=0, keepdims=True)


def input_grad_body(*refs):
    piece_refs = refs[:-6]
    grad_ref, token_ref, inverse_ref, gain_ref, sum_ref, out_ref = refs[-6:]
    _, width = grad_ref.shape
    inverse = inverse_ref[...]
    token_sums = row_as_columns(sum_ref[...], width)
    model_width = width * lax.axis_size("mp")
    out_ref[...] = (
        grad_ref[...]
        + inverse * gain_ref[...] * summed(piece_refs)
        - token_ref[...].astype(F32) * (inverse * inverse / model_width * token_sums)
    )


def second_half_body(*refs):
    count = (len(refs) - 18) // 2
    chunk_refs = refs[:count]
    (
        out_full_ref,
        q_ref,
        k_ref,
        v_ref,
        lse_ref,
        proj_ref,
        factor_ref,
        cos_ref,
        sin_ref,
        segr_ref,
        segc_ref,
        full_ref,
    ) = refs[count : count + 12]
    all_ref, g_ref, scale_ref, token_ref = refs[count + 12 : count + 16]
    part_refs = refs[count + 16 : -2]
    mixed_ref, sum_ref = refs[-2:]
    tokens, width = chunk_refs[0].shape
    heads = width // HD
    for k, ref in enumerate(chunk_refs):
        all_ref[:, k * width : (k + 1) * width] = ref[...]
    mixed_grads = dot(all_ref[...], out_full_ref[...], 1, 1).astype(LOW)
    cosine = cos_ref[...]
    sine = sin_ref[...]
    mixed_ref[...] = mixed_grads
    sum_ref[...] = jnp.zeros_like(sum_ref)

    def one_head(head, carry):
        at = pl.ds(pl.multiple_of(head * HD, HD), HD)
        query_grads, key_grads, value_grads = [], [], []
        for rows, seen in query_blocks(tokens):
            mixed_grad = mixed_ref[rows, at]
            logits = masked_logits(q_ref, k_ref, segr_ref, segc_ref, at, rows, seen)
            probs = jnp.exp(logits - lse_ref[head, rows, :])
            prob_grad = dot(mixed_grad, v_ref[seen, at], 1, 1)
            delta = jnp.sum(prob_grad * probs, axis=1, keepdims=True)
            raw_grad = (probs * (prob_grad - delta) * HD ** (-0.5)).astype(LOW)
            query_grads.append(dot(raw_grad, k_ref[seen, at]))
            key_grads.append(dot(raw_grad, q_ref[rows, at], 0, 0))
            value_grads.append(dot(probs.astype(LOW), mixed_grad, 0, 0))

        def joined(parts):
            size = parts[0].shape[0]
            return jnp.concatenate([parts[0] + parts[1][:size], parts[1][size:]], axis=0)

        query_grad = jnp.concatenate(query_grads, axis=0)
        key_grad = joined(key_grads)
        grads = (
            query_grad * cosine - halves_turned(query_grad) * sine,
            key_grad * cosine - halves_turned(key_grad) * sine,
            joined(value_grads),
        )
        for member in range(3):
            lanes = pl.ds(pl.multiple_of(member * width + head * HD, HD), HD)
            shaped = proj_ref[:, lanes]
            lowered = (grads[member] * factor_ref[:, lanes]).astype(LOW)
            g_ref[:, lanes] = lowered
            scale_ref[:, lanes] = jnp.sum(grads[member] * shaped, axis=0, keepdims=True)
            sum_ref[...] += lowered.astype(F32) * shaped
        return carry

    lax.fori_loop(0, heads, one_head, 0)
    token_total = sum_ref[...]
    token_ref[...] = lane_sums_as_row(token_total)
    for k, ref in enumerate(part_refs):
        ref[...] = dot(g_ref[...], full_ref[k * width : (k + 1) * width, :], 1, 1).astype(LOW)


def put_bundles(refs, rows, values):
    inner = len(refs)
    width = refs[0].shape[2]
    for b, ref in enumerate(refs):
        for a in range(PLANES):
            at = (a * inner + b) * width
            ref[a, rows, :] = values[:, at : at + width].astype(LOW)


def negative_ratio(scale, magnitude, square):
    norm = jnp.sqrt(jnp.where(square == 0.0, 1.0, square))
    return -scale * magnitude / (norm * norm * norm)


def column_adapters(
    low_grad, inputs, inner, inverse, full, square, magnitude, scale, lefts, rights, members
):
    half = rights.shape[0] // 2
    high = rights[:half]
    ratio = negative_ratio(scale, magnitude, square)
    rank = dot(low_grad, high, 1, 1)
    if inverse is not None:
        rank = rank * inverse
        inner = inner * inverse
    left_part = dot(rank.astype(LOW), inputs, 0, 0) + dot(
        (high.astype(F32) * ratio).astype(LOW), full, 1, 1
    )
    right_part = dot(inner.astype(LOW), low_grad, 0, 0) + ratio * dot(lefts[:half], full)
    size = low_grad.shape[1] // members
    rights_out = [
        right_part[slot * R : (slot + 1) * R, slot * size : (slot + 1) * size]
        for slot in range(members)
    ]
    return SCALE * left_part, rights_out


def two_adapters_body(
    low_ref,
    scaled_ref,
    inverse_ref,
    full_ref,
    square_ref,
    magnitude_ref,
    scale_ref,
    left_ref,
    right_ref,
    broad_ref,
    *bundle_refs,
):
    hidden = broad_ref.shape[1]
    left_part, rights_out = column_adapters(
        low_ref[...],
        scaled_ref[...],
        dot(scaled_ref[...], left_ref[...], 1, 1),
        inverse_ref[...],
        full_ref[...],
        square_ref[...],
        magnitude_ref[...],
        scale_ref[...],
        left_ref[...],
        right_ref[...],
        2,
    )
    put_bundles(bundle_refs, slice(None), left_part)
    broad_ref[:R, :] = rights_out[0]
    broad_ref[R : 2 * R, :] = rights_out[1]
    broad_ref[2 * R : 2 * R + 1, :] = scale_ref[:, :hidden]
    broad_ref[2 * R + 1 : 2 * R + 2, :] = scale_ref[:, hidden:]
    broad_ref[2 * R + 2 :, :] = jnp.zeros((6, hidden), F32)


def row_adapters(grads, inputs, high, left_rows):
    rank = dot(grads, high, 1, 1)
    left_part = SCALE * dot(rank.astype(LOW), inputs, 0, 0)
    inner = dot(inputs, left_rows, 1, 1)
    return left_part, dot(inner.astype(LOW), grads, 0, 0)


def ratio_adapters_body(
    out_high_ref, out_full_ref, down_high_ref, down_full_ref, ratio_ref, rows_ref
):
    width = rows_ref.shape[1]
    for slot, (high_ref, full_ref) in enumerate(
        ((out_high_ref, out_full_ref), (down_high_ref, down_full_ref))
    ):
        scaled = (high_ref[...].astype(F32) * ratio_ref[slot : slot + 1, :]).astype(LOW)
        part = SCALE * dot(scaled, full_ref[...], 1, 1)
        for first in range(0, part.shape[1], width):
            at = slot * R + first // width * R
            rows_ref[at : at + R, :] = part[:, first : first + width]


def end_adapters_body(*refs):
    (
        low_ref,
        normed_ref,
        inner_ref,
        full_ref,
        square_ref,
        magnitude_ref,
        scale_ref,
        left_ref,
        right_ref,
        gout_ref,
        mixed_ref,
        out_high_ref,
        out_left_ref,
        gdown_ref,
        act_ref,
        down_high_ref,
        down_left_ref,
    ) = refs[:17]
    inner = (len(refs) - 18) // 4
    moved_refs, rows_ref, bundle_refs = refs[17:-inner - 1], refs[-inner - 1], refs[-inner:]
    for b, ref in enumerate(bundle_refs):
        ref[:, 5 * R : 7 * R, :] = moved_refs[b][...]
        ref[:, 7 * R : 8 * R, :] = moved_refs[inner + b][...]
        ref[:, 8 * R :, :] = moved_refs[2 * inner + b][...]
    width = rows_ref.shape[1]
    left_part, rights_out = column_adapters(
        low_ref[...],
        normed_ref[...],
        inner_ref[...],
        None,
        full_ref[...],
        square_ref[...],
        magnitude_ref[...],
        scale_ref[...],
        left_ref[...],
        right_ref[...],
        3,
    )
    put_bundles(bundle_refs, slice(0, 3 * R), left_part)
    left_out, right_out = row_adapters(
        gout_ref[...],
        mixed_ref[...],
        out_high_ref[...],
        out_left_ref[:R, :],
    )
    put_bundles(bundle_refs, slice(3 * R, 4 * R), right_out)
    left_down, right_down = row_adapters(
        gdown_ref[...],
        act_ref[...],
        down_high_ref[...],
        down_left_ref[:R, :],
    )
    put_bundles(bundle_refs, slice(4 * R, 5 * R), right_down)
    at = 0
    for values in rights_out + [left_out]:
        rows_ref[at : at + R, :] = values
        at += R
    for first in range(0, left_down.shape[1], width):
        rows_ref[at : at + R, :] = left_down[:, first : first + width]
        at += R
    for slot in range(3):
        rows_ref[at + slot : at + slot + 1, :] = scale_ref[:, slot * width : (slot + 1) * width]
    rows_ref[at + 3 : at + 8, :] = jnp.zeros((5, width), F32)


def statistics_body(*refs):
    out_ref = refs[-1]
    lanes = lax.broadcasted_iota(jnp.int32, out_ref.shape, 1)
    table = jnp.zeros(out_ref.shape, F32)
    member = 0
    for slot, members in enumerate((3, 1, 2, 1)):
        norms = jnp.sqrt(refs[2 * slot][...])
        drifts = refs[2 * slot + 1][...] - norms
        size = norms.shape[1] // members
        for part in range(members):
            taken = slice(part * size, (part + 1) * size)
            norm, drift = norms[:, taken], drifts[:, taken]
            first = jnp.sum(drift * drift, axis=1, keepdims=True)
            second = jnp.sum(norm, axis=1, keepdims=True)
            table = jnp.where(lanes == member, first, table)
            table = jnp.where(lanes == member + 7, second, table)
            member += 1
    out_ref[...] = table


def on_device(
    tokens,
    cotangent,
    segment_ids,
    attention_gain,
    feedforward_gain,
    *parameters,
):
    count = lax.axis_size("mp")
    inner_count = count // PLANES
    place = lax.axis_index("mp")
    scalars = jnp.stack([place, lax.axis_index("dp")]).astype(jnp.int32)
    weights = parameters[:7]
    lefts = parameters[7::3]
    rights = parameters[8::3]
    magnitudes = parameters[9::3]
    token_count, width = tokens.shape
    hidden = weights[4].shape[1] // count
    hidden_padded = round_up(hidden)
    widths = [weight.shape[1] // count for weight in weights]
    chunk_shape = (token_count, width)
    rights_one, rights_two, magnitude_one, magnitude_two, magnitude_out, magnitude_down = (
        own_factors(rights, magnitudes, width, hidden, hidden_padded, scalars)
    )

    def scaled_lefts(members):
        return SCALE * jnp.concatenate([lefts[member].T for member in members], axis=0)

    own_one, *blocks_one = cut_blocks(weights[:3], width, width, scalars)
    extended = jnp.concatenate(
        [
            tokens,
            split_rows(scaled_lefts((0, 1, 2))),
            scaled_lefts((4, 5)).astype(LOW),
            attention_gain[None],
            feedforward_gain[None],
            jnp.zeros((14, width), LOW),
        ],
        axis=0,
    )
    token_chunks = gather(extended)
    pieces_one = exchanged(blocks_one)
    lefts_one, lefts_two, gain_two_all = gathered_lefts(token_chunks, token_count)
    weight_one, full_one, squares_one = assemble(
        own_one, pieces_one, lefts_one, rights_one, scalars, True
    )

    length = segment_ids.shape[1]
    key_index = jnp.arange(length, dtype=jnp.int32)
    segments = segment_ids[0]
    change = jnp.concatenate(
        [jnp.ones((1,), jnp.int32), (segments[1:] != segments[:-1]).astype(jnp.int32)]
    )
    places = (key_index - lax.cummax(key_index * change, axis=0)).astype(F32)
    half = HD // 2
    freqs = THETA ** (-2.0 * jnp.arange(half, dtype=F32) / HD)
    angles = places[:, None] * freqs[None, :]
    cosine = jnp.cos(angles)
    sine = jnp.sin(angles)
    cosine = jnp.concatenate([cosine, cosine], axis=1)
    sine = jnp.concatenate([-sine, sine], axis=1)
    seg_rows = segments[:, None]
    seg_cols = segments[None, :]

    left_out = split_rows(scaled_lefts((3,)))
    left_down = pad_to(split_rows(scaled_lefts((6,))), hidden_padded, 1)
    full_out, high_out, squares_out, _, *cross_out = row_block(
        weights[3], left_out, rights[3], magnitudes[3][None], width, width, scalars
    )
    full_down, high_down, squares_down, magnitude_down_all, *cross_down = row_block(
        weights[6], left_down, rights[6], magnitudes[6][None], width, hidden_padded, scalars
    )
    squares_all, _ = total_relative(
        jnp.concatenate([squares_out, squares_down], axis=0)
        .reshape(2, count, width)
        .transpose(1, 0, 2)
        .reshape(count, 2 * width),
        jnp.zeros((0, 2 * width), F32),
    )
    square_out, square_down = squares_all[:1, :width], squares_all[:1, width:]
    square_down_all = squares_all[:, width:].reshape(1, count * width)
    factor_out = magnitude_out / jnp.sqrt(square_out)
    factor_down = magnitude_down / jnp.sqrt(square_down)

    heads = width // HD
    (
        normed_one,
        proj_one,
        inner_one,
        queries,
        keys,
        values,
        mixed,
        log_totals,
        inverse_one,
        factor_one,
        *parts_out,
    ) = kernel(
        first_half_body,
        [
            ((token_count, count * width), LOW),
            ((token_count, 3 * width), F32),
            ((token_count, 3 * R), F32),
        ]
        + [(chunk_shape, LOW)] * 4
        + [((heads, token_count, 1), F32), ((token_count, 1), F32), ((1, 3 * width), F32)]
        + [(chunk_shape, LOW)] * count,
        *token_chunks,
        weight_one,
        squares_one,
        magnitude_one,
        lefts_one,
        rights_one,
        cosine,
        sine,
        seg_rows,
        seg_cols,
        full_out,
    )
    gain_one = attention_gain.astype(F32)[None]
    gain_two = feedforward_gain.astype(F32)[None]
    shaped_out, middle, chunk_two = kernel(
        middle_body,
        [(chunk_shape, F32), (chunk_shape, F32), (chunk_shape, LOW)],
        *scatter_pieces(parts_out),
        tokens,
        gain_two,
        factor_out,
    )

    cotangent_chunks = gather(cotangent)
    grad_down_all, grad_activated = kernel(
        down_grad_body,
        [((token_count, count * width), LOW), ((token_count, hidden_padded), F32)],
        *cotangent_chunks,
        square_down_all,
        magnitude_down_all,
        full_down,
    )
    own_two, *blocks_two = cut_blocks(weights[4:6], hidden, hidden_padded, scalars)
    full_two, squares_two = assemble(
        own_two, exchanged(blocks_two), lefts_two, rights_two, scalars, False
    )

    scaled_two, inverse_two, activated, low_two, scale_two, token_two, *parts_two = by_rows(
        feed_forward_body,
        2,
        count,
        (count + 4,),
        (4,),
        5,
        [
            ((token_count, count * width), LOW),
            ((token_count, 1), F32),
            ((token_count, hidden_padded), LOW),
            ((token_count, 2 * hidden_padded), LOW),
            ((1, 2 * hidden_padded), F32),
            ((1, token_count), F32),
        ]
        + [(chunk_shape, LOW)] * count,
        *gather(chunk_two),
        gain_two_all,
        full_two,
        squares_two,
        magnitude_two,
        grad_activated,
    )
    token_two = total_over(token_two, "mp")
    grad_middle, grad_out, scale_out = kernel(
        grad_middle_body,
        [(chunk_shape, F32), (chunk_shape, LOW), ((1, width), F32)],
        *scatter_pieces(parts_two),
        cotangent,
        middle,
        inverse_two,
        gain_two,
        token_two,
        factor_out,
        shaped_out,
    )
    parts_down = by_rows(
        down_body, 2, 1, (), (), None, [(chunk_shape, LOW)] * count, activated, full_down
    )
    layer_out, scale_down = kernel(
        result_body,
        [(chunk_shape, LOW), ((1, width), F32)],
        *scatter_pieces(parts_down),
        middle,
        cotangent,
        factor_down,
    )

    grad_out_all, low_one, scale_one, token_one, *parts_one = kernel(
        second_half_body,
        [
            ((token_count, count * width), LOW),
            ((token_count, 3 * width), LOW),
            ((1, 3 * width), F32),
            ((1, token_count), F32),
        ]
        + [(chunk_shape, LOW)] * count,
        *gather(grad_out),
        full_out,
        queries,
        keys,
        values,
        log_totals,
        proj_one,
        factor_one,
        cosine,
        sine,
        seg_rows,
        seg_cols,
        full_one,
        scratch=[pltpu.VMEM(chunk_shape, LOW), pltpu.VMEM((token_count, HD), F32)],
    )
    (stat_row,) = kernel(
        statistics_body,
        [((1, token_count), F32)],
        squares_one,
        magnitude_one,
        square_out,
        magnitude_out,
        squares_two,
        magnitude_two,
        square_down,
        magnitude_down,
    )
    own_ratios = jnp.concatenate(
        [
            negative_ratio(scale_out, magnitude_out, square_out),
            negative_ratio(scale_down, magnitude_down, square_down),
        ],
        axis=1,
    )
    rows_wide = max(2 * width, token_count)
    ratios_all, totals = total_relative(
        pad_to(pad_to(own_ratios, count, 0), rows_wide, 1),
        pad_to(jnp.concatenate([token_one, stat_row], axis=0), rows_wide, 1),
    )
    token_one = totals[:1, :token_count]
    ratio_rows = jnp.concatenate(
        [
            ratios_all[:, slot * width : (slot + 1) * width].reshape(1, count * width)
            for slot in range(2)
        ],
        axis=0,
    )
    (input_gradient,) = kernel(
        input_grad_body,
        [(chunk_shape, F32)],
        *scatter_pieces(parts_one),
        grad_middle,
        tokens,
        inverse_one,
        gain_one,
        token_one,
    )

    broad, *bundles = kernel(
        two_adapters_body,
        [((2 * R + 8, hidden_padded), F32)] + [((PLANES, 2 * R, width), LOW)] * inner_count,
        low_two,
        scaled_two,
        inverse_two,
        full_two,
        squares_two,
        magnitude_two,
        scale_two,
        lefts_two,
        rights_two,
    )
    broad = total_over(broad, "dp")

    slabs = hidden_padded // width
    rows_end, *bundles_end = kernel(
        end_adapters_body,
        [(((4 + slabs) * R + 8, width), F32)] + [((PLANES, 9 * R, width), LOW)] * inner_count,
        low_one,
        normed_one,
        inner_one,
        full_one,
        squares_one,
        magnitude_one,
        scale_one,
        lefts_one,
        rights_one,
        grad_out_all,
        mixed,
        high_out,
        left_out,
        grad_down_all,
        activated,
        high_down,
        left_down,
        *bundles,
        *cross_out,
        *cross_down,
    )
    spread = small_scatter(bundles_end)
    crossed = spread[7 * R :]
    (rows_ratio,) = kernel(
        ratio_adapters_body,
        [(((1 + slabs) * R, width), F32)],
        high_out,
        full_out,
        high_down,
        full_down,
        ratio_rows,
    )
    last = total_over(
        jnp.concatenate(
            [
                spread[: 7 * R],
                rows_end[: 3 * R],
                rows_end[3 * R : (4 + slabs) * R] + rows_ratio,
                rows_end[(4 + slabs) * R :][:3],
                scale_out,
                scale_down,
                jnp.zeros((3, width), F32),
            ],
            axis=0,
        ),
        "dp",
    )

    own_square = [squares_one[:, slot * width : (slot + 1) * width] for slot in range(3)] + [
        square_out,
        squares_two[:, :hidden_padded],
        squares_two[:, hidden_padded:],
        square_down,
    ]
    stat_sums = jnp.stack([totals[1, :7], totals[1, 7:14]], axis=1)
    columns_all = jnp.array([weight.shape[1] for weight in weights], F32)[:, None]
    means = stat_sums / columns_all
    statistics = jnp.concatenate([jnp.sqrt(means[:, :1]), means[:, 1:]], axis=1)

    def rows_of(values, slot):
        return values[slot * R : (slot + 1) * R]

    scales_at = (11 + slabs) * R
    right_ends = [
        rows_of(last, 3 + slot)
        + negative_ratio(last[scales_at + 3 + slot][None], magnitude, square)
        * rows_of(crossed, slot)
        for slot, magnitude, square in (
            (0, magnitude_out, square_out),
            (1, magnitude_down, square_down),
        )
    ]
    down_rows = jnp.concatenate([rows_of(last, 11 + slab) for slab in range(slabs)], axis=1)
    left_grads = [rows_of(last, slot).T for slot in range(3)] + [
        rows_of(last, 10).T,
        rows_of(last, 5).T,
        rows_of(last, 6).T,
        down_rows[:, :hidden].T,
    ]
    right_grads = [rows_of(last, 7 + slot) for slot in range(3)] + [
        right_ends[0],
        rows_of(broad, 0)[:, :hidden],
        rows_of(broad, 1)[:, :hidden],
        right_ends[1],
    ]
    scale_grads = [last[scales_at + slot] for slot in range(4)] + [
        broad[2 * R, :hidden],
        broad[2 * R + 1, :hidden],
        last[scales_at + 4],
    ]
    results = [layer_out, input_gradient]
    for member in range(7):
        results += [
            left_grads[member],
            right_grads[member],
            scale_grads[member] / jnp.sqrt(own_square[member][0, : widths[member]]),
        ]
    return tuple(results + [statistics])


def solution(mesh):
    grid = P("dp", "mp")
    rows = P("mp", None)
    placed = (grid, grid, P("dp", None), P("mp"), P("mp")) + (rows,) * 7 + (rows, P(), P()) * 7
    adapters = (rows, P(None, "mp"), P("mp")) * 7
    return jax.shard_map(
        on_device,
        mesh=mesh,
        in_specs=placed,
        out_specs=(grid, grid) + adapters + (P(),),
        check_vma=False,
    )
```
